32 devices in a mesh: len: 8 (over z, y), wire: 4 (over x, core).
Axes of the slice: x: 2, y: 2, z: 4, core: 2. Of those that a mesh axis runs over, the one named last changes fastest.
Arguments:
- displacement: float32 [8, 4, 3, 3584], P('len', 'wire'), may hold values from -6 to 6
- previous: float32 [8, 4, 3, 3584], P('len', 'wire'), may hold values from -6 to 6
- element_nodes: int32 [8, 4, 125, 64], P('len', 'wire'), may hold values from 0 to 223
- element_stiffness: float32 [8, 4, 64], P('len', 'wire'), may hold values from 0.5 to 2
- gradient_op: float32 [375, 125], replicated, may hold values from -0.5 to 0.5
- mass_partial: float32 [8, 4, 3584], P('len', 'wire'), may hold values from 0.5 to 2
- left_ghost: int32 [8, 4, 768], P('len', 'wire'), may hold values from 0 to 3583, as said below
- right_ghost: int32 [8, 4, 768], P('len', 'wire'), may hold values from 0 to 3583, as said below
- contact_slots: int32 [8, 4, 4, 2048], P('len', 'wire'), may hold values from 0 to 3583
- contact_live: int32 [8, 4, 4, 2048], P('len', 'wire'), may hold values from 0 to 1, as said below
Outputs:
- final_field: float32 [8, 4, 3, 3584], P('len', 'wire')
- prior_field: float32 [8, 4, 3, 3584], P('len', 'wire')
The draws below stay inside these ranges and needn't reach their ends.
Inputs may be any that keep to these rules, and one draw needn't show every extreme that they name: Within one piece the 768 slots of left_ghost and the 768 slots of right_ghost are all distinct. Within one piece the 768 slots of right_ghost and those of left_ghost are all distinct. contact_live[l, w, q, k] equals contact_live[l, q, w, k], and is 0 where q = w.
All inputs are finite; a program needn't handle non-finite values.
Results may differ from the reference program's by a relative error of at most 0.0003.
Values sent between devices are 32-bit elements; how exact they have to be, the bound alone decides.
A program may use at most 64 MiB of HBM per device.

```python
import math
import jax
import jax.numpy as jnp
from jax import lax

NPE = 125
E_DEV = 64
GHOST = 768
CPAIR = 2048
ITERS = 4
NODES = 3584
NGRAD = 375
SEGS = 8
WIRES = 4


def shuffled_slots(key):
    device_keys = jax.random.split(jax.random.fold_in(key, 11), SEGS * WIRES)
    shuffled = jax.vmap(lambda one_key: jax.random.permutation(one_key, NODES))(device_keys)
    return shuffled.reshape(SEGS, WIRES, NODES)


def draw_left_ghost(key, part):
    return shuffled_slots(key)[:, :, :GHOST].astype(jnp.int32)


def draw_right_ghost(key, part):
    return shuffled_slots(key)[:, :, GHOST:2 * GHOST].astype(jnp.int32)


def draw_contact_live(key, part):
    rate_key, bits_key = jax.random.split(jax.random.fold_in(key, 23))
    live_rate = jax.random.randint(rate_key, (SEGS, WIRES, WIRES, 1), 20, 101)
    random_bits = jax.random.randint(bits_key, (SEGS, WIRES, WIRES, CPAIR), 0, 100)
    upper_half = (random_bits < live_rate).astype(jnp.int32)
    mirrored = jnp.transpose(upper_half, (0, 2, 1, 3))
    wire_ids = jnp.arange(WIRES)
    above_diag = (wire_ids[:, None] < wire_ids[None, :])[None, :, :, None]
    below_diag = (wire_ids[:, None] > wire_ids[None, :])[None, :, :, None]
    return jnp.where(above_diag, upper_half, jnp.where(below_diag, mirrored, 0)).astype(jnp.int32)


def with_ends(drawn, rng, least, high):
    shape = drawn.shape
    place = [jax.random.randint(jax.random.fold_in(rng, axis), (), 0, shape[axis]) for axis in range(len(shape))]
    drawn = drawn.at[tuple(place)].set(least)
    longest = shape.index(max(shape))
    place[longest] = (place[longest] + 1) % shape[longest]
    return drawn.at[tuple(place)].set(high)


def shard_levels(key, extent, pieces, low, largest):
    factor_of, own = 1.0, jax.random.fold_in(key, 6)
    for position, parts in pieces:
        heights = jnp.exp(jax.random.uniform(jax.random.fold_in(own, position), (parts,), jnp.float32, low / len(pieces), largest / len(pieces)))
        factor_of = factor_of * jnp.repeat(heights, extent[position] // parts).reshape([-1 if axis == position else 1 for axis in range(len(extent))])
    return factor_of


def scatter_about(key, extent, scale, limit, cuts=(), kind=jnp.bfloat16):
    entries = scale * jax.random.normal(key, extent, jnp.float32)
    if cuts:
        entries = entries * shard_levels(key, extent, cuts, -0.22, 0.18)
    return jnp.clip(entries, -limit, limit).astype(kind)


def setup_inputs(seed: int = 0) -> dict:
    seeds = jax.random.split(jax.random.key(seed), 11)
    return {
        "displacement": scatter_about(seeds[0], (SEGS, WIRES, 3, NODES), 1.0, 6.0, ((0, 8), (1, 4)), jnp.float32),
        "previous": scatter_about(seeds[1], (SEGS, WIRES, 3, NODES), 1.0, 6.0, ((0, 8), (1, 4)), jnp.float32),
        "element_nodes": with_ends(jax.random.randint(seeds[2], (SEGS, WIRES, NPE, E_DEV), 0, 224), jax.random.fold_in(seeds[2], 1), 0, 223).astype(jnp.int32),
        "element_stiffness": jnp.clip(jnp.exp(math.log(2.0) - 1.3862944 * jax.random.uniform(seeds[3], (SEGS, WIRES, E_DEV), jnp.float32) ** shard_levels(seeds[3], (SEGS, WIRES, E_DEV), ((0, 8), (1, 4)), -0.2, 0.2)), 0.5, 2.0),
        "gradient_op": scatter_about(seeds[4], (NGRAD, NPE), NPE ** -0.5, 0.5, (), jnp.float32),
        "mass_partial": jnp.clip(jnp.exp(math.log(2.0) - 1.3862944 * jax.random.uniform(seeds[5], (SEGS, WIRES, NODES), jnp.float32) ** shard_levels(seeds[5], (SEGS, WIRES, NODES), ((0, 8), (1, 4)), -0.2, 0.2)), 0.5, 2.0),
        "left_ghost": draw_left_ghost(jax.random.fold_in(seeds[10], 71), 0),
        "right_ghost": draw_right_ghost(jax.random.fold_in(seeds[10], 71), 0),
        "contact_slots": with_ends(jax.random.randint(seeds[8], (SEGS, WIRES, WIRES, CPAIR), 0, NODES), jax.random.fold_in(seeds[8], 1), 0, NODES - 1).astype(jnp.int32),
        "contact_live": draw_contact_live(jax.random.fold_in(seeds[10], 71), 0),
    }


PENALTY = 4.0
TIME_SQUARE = 0.03
block_elements = 4
block_slots = 224


def take_slots(field, slots):
    return field[:, slots]


def add_slots(field, slots, values):
    return field.at[:, slots].add(values)


def element_force(field, local_nodes, stiffness, gradient_op):
    offsets = (jnp.arange(local_nodes.shape[1], dtype=jnp.int32) // block_elements) * block_slots
    nodes = (local_nodes + offsets[None, :]).astype(jnp.int32)
    element_field = field[:, nodes]
    gradients = jnp.einsum("gn,cne->cge", gradient_op, element_field, precision=lax.Precision.HIGHEST)
    stresses = gradients * stiffness[None, None, :]
    element_out = jnp.einsum("gn,cge->cne", gradient_op, stresses, precision=lax.Precision.HIGHEST)
    return jnp.zeros_like(field).at[:, nodes].add(-element_out)


def assemble(partial_value, left_ghost, right_ghost):
    take_all = jax.vmap(jax.vmap(take_slots))
    add_all = jax.vmap(jax.vmap(add_slots))
    left_send = take_all(partial_value, left_ghost)
    right_send = take_all(partial_value, right_ghost)
    blank = jnp.zeros_like(left_send[:1])
    from_prev = jnp.concatenate([blank, right_send[:-1]], axis=0)
    from_next = jnp.concatenate([left_send[1:], blank], axis=0)
    partial_value = add_all(partial_value, left_ghost, from_prev)
    return add_all(partial_value, right_ghost, from_next)


def reference(displacement, previous, element_nodes, element_stiffness, gradient_op, mass_partial, left_ghost, right_ghost, contact_slots, contact_live):
    mass = assemble(mass_partial[:, :, None, :], left_ghost, right_ghost)
    flat_slots = contact_slots.reshape(SEGS, WIRES, WIRES * CPAIR)
    live = contact_live.astype(jnp.float32)[:, :, None, :, :]
    per_wire = jax.vmap(element_force, in_axes=(0, 0, 0, None))

    def segment_force(group):
        return per_wire(group[0], group[1], group[2], gradient_op)

    for turn_index in range(ITERS):
        force = lax.map(segment_force, (displacement, element_nodes, element_stiffness))
        sent = jax.vmap(jax.vmap(take_slots))(displacement, flat_slots).reshape(SEGS, WIRES, 3, WIRES, CPAIR)
        received = jnp.transpose(sent, (0, 3, 2, 1, 4))
        penalty = (PENALTY * live * (received - sent)).reshape(SEGS, WIRES, 3, WIRES * CPAIR)
        force = jax.vmap(jax.vmap(add_slots))(force, flat_slots, penalty)
        force = assemble(force, left_ghost, right_ghost)
        stepped = 2.0 * displacement - previous + TIME_SQUARE * force / mass
        previous, displacement = displacement, stepped
    return displacement, previous
```

```python
import functools

import jax
import jax.numpy as jnp
from jax import lax
from jax.experimental import pallas as pl
from jax.experimental.pallas import tpu as pltpu
from jax.sharding import PartitionSpec as P

ITERS = 4
PENALTY = 4.0
TIME_SQUARE = 0.03
block_slots = 224
block_elements = 4
LANES = 128
ARGS = 10
VMEM_BYTES = 67_043_328
FIRST = (8, 9, 0)
LATER = (1, 2, 3, 4, 5, 6, 7)
BLOCK_SCALE, BLOCK_SHIFT = 4682, 20
SUB = 8
f32 = jnp.float32
bf16 = jnp.bfloat16
MESH = pl.DeviceIdType.MESH


def round_up(value, step):
    return -(-value // step) * step


def dot(a, b):
    return jnp.dot(a, b, preferred_element_type=f32)


def lane_take(values, lanes):
    return jnp.take_along_axis(values, lanes, axis=1, mode="promise_in_bounds")


def step_kernel(
    wires,
    segments,
    chunk,
    *refs,
):
    sources, refs = refs[:ARGS], refs[ARGS:]
    inputs, in_sem, refs = refs[2 : 2 + ARGS], refs[2 + ARGS], refs[:2] + refs[3 + ARGS :]
    copies = [
        pltpu.make_async_copy(source, target, in_sem.at[i])
        for i, (source, target) in enumerate(zip(sources, inputs))
    ]
    for i in FIRST + LATER:
        copies[i].start()
    run(wires, segments, chunk, copies, *inputs, *refs)


def run(
    wires,
    segments,
    chunk,
    copies,
    u_in, p_in, nodes_in, stiff_in, grad_in, mass_in, left_in, right_in, slots_in, live_in,
    u_out, p_out,
    u_ref, p_ref, mass_ref, rate_ref,
    c_hot, g_hot, c_back, g_back, e_back, cb_ref, gb_ref, gram, nodes_ref, lists_ref, stiff_ref, scale_ref,
    part, field, c_send, c_recv, g_send, g_recv,
    c_ssem, c_rsem, g_ssem, g_rsem,
):
    others = wires - 1
    blocks = e_back.shape[0]
    parts = u_in.shape[1]
    rows, wide = u_ref.shape
    pairs = slots_in.shape[3]
    ghosts = left_in.shape[2]
    elements, node_count = nodes_in.shape[2:]
    node_pad = gram.shape[0] // 2
    contact_row = elements
    ghost_row = contact_row + others * pairs // LANES
    me = lax.axis_index("wire")
    seg = lax.axis_index("len")
    has_prev = seg > 0
    has_next = seg < segments - 1
    mirrored = wires & (wires - 1) == 0

    def partner(d):
        if not mirrored:
            return lax.rem(me + (d + 1), wires)
        offset, other, bit = wires - 1 - d, me, 1
        while bit <= offset:
            if offset & bit:
                other = other + bit - 2 * bit * lax.rem(lax.div(me, bit), 2)
            bit *= 2
        return other

    def landing(d):
        return d if mirrored else others - 1 - d

    barrier = pltpu.get_barrier_semaphore()
    for d in range(others):
        pl.semaphore_signal(barrier, inc=1, device_id={"wire": partner(d)}, device_id_type=MESH)

    @pl.when(has_prev)
    def _():
        pl.semaphore_signal(barrier, inc=1, device_id={"len": seg - 1}, device_id_type=MESH)

    @pl.when(has_next)
    def _():
        pl.semaphore_signal(barrier, inc=1, device_id={"len": seg + 1}, device_id_type=MESH)

    def rows_of(width):
        return lax.broadcasted_iota(jnp.int32, (SUB, width), 0)

    def doubled(x):
        return x + pltpu.roll(x, 4, 0)

    def match(slots):
        ids = lax.broadcasted_iota(jnp.int32, (wide, LANES), 0).astype(bf16)
        here = jnp.broadcast_to(slots.astype(f32), (2 * SUB, LANES)).astype(bf16)
        here = jnp.concatenate([here] * (wide // (2 * SUB)), axis=0)
        return jnp.where(ids == here, jnp.ones((), bf16), jnp.zeros((), bf16))

    def block_of(slots):
        return (slots * BLOCK_SCALE) >> BLOCK_SHIFT

    def spread_columns(columns, at):
        lanes = lax.broadcasted_iota(jnp.int32, (LANES, wide), 1).astype(bf16)
        here = jnp.broadcast_to(columns[:, at : at + 1], (LANES, wide))
        return jnp.where(lanes == here, jnp.ones((), bf16), jnp.zeros((), bf16))

    def fill(hot, base_ref, at, slots, live, row):
        count = slots.shape[1]
        which = block_of(slots)
        inside = slots - which * block_slots
        if live is not None:
            which = jnp.where(live > 0, which, -1)
        base_ref[:, at : at + count] = jnp.broadcast_to(which, (SUB, count))
        for start in range(0, count, LANES):
            here = inside[:, start : start + LANES]
            group, lane = divmod(at + start, hot.shape[2])
            hot[group, :, lane : lane + LANES] = match(here)
            at_row = row + (at + start) // LANES
            lists_ref[at_row : at_row + 1, :] = here.astype(f32)

    for i in FIRST:
        copies[i].wait()
    u_ref[...] = jnp.zeros_like(u_ref)
    p_ref[...] = jnp.zeros_like(p_ref)
    lists_ref[...] = jnp.zeros_like(lists_ref)
    for b in range(blocks):
        lanes = slice(b * block_slots, (b + 1) * block_slots)
        for c in range(parts):
            row = slice(b * SUB + c, b * SUB + c + 1)
            u_ref[row, :block_slots] = u_in[0, c, :, lanes]
        at = slice(b * SUB, (b + 1) * SUB)
        u_ref[at, :] = doubled(u_ref[at, :])
    for d in range(others):
        fill(c_hot, cb_ref, d * pairs, slots_in[0, 0, pl.ds(partner(d), 1), :], live_in[0, 0, pl.ds(partner(d), 1), :], contact_row)

    @pl.when(jnp.logical_not(has_prev))
    def _():
        g_recv[:, 0] = jnp.zeros((ITERS,) + g_recv.shape[2:], f32)

    @pl.when(jnp.logical_not(has_next))
    def _():
        g_recv[:, 1] = jnp.zeros((ITERS,) + g_recv.shape[2:], f32)

    def prepare():
        for i in LATER:
            copies[i].wait()
        mass_ref[...] = jnp.zeros_like(mass_ref)
        for b in range(blocks):
            at = slice(b * SUB, (b + 1) * SUB)
            lanes = slice(b * block_slots, (b + 1) * block_slots)
            for c in range(parts):
                p_ref[b * SUB + c : b * SUB + c + 1, :block_slots] = p_in[0, c, :, lanes]
            p_ref[at, :] = doubled(p_ref[at, :])
            mass_ref[b * SUB + 3 : b * SUB + 4, :] = jnp.ones((1, wide), f32)
            mass_ref[b * SUB + 3 : b * SUB + 4, :block_slots] = mass_in[0, :, lanes]
            mass_ref[at, :] = doubled(mass_ref[at, :])
        fill(g_hot, gb_ref, 0, left_in[0], None, ghost_row)
        fill(g_hot, gb_ref, ghosts, right_in[0], None, ghost_row)
        op = grad_in[...]
        product = lax.dot_general(
            op, op, (((0,), (0,)), ((), ())), precision=lax.Precision.HIGHEST, preferred_element_type=f32
        )
        high = product.astype(bf16)
        low = (product - high.astype(f32)).astype(bf16)
        gram[...] = jnp.zeros_like(gram)
        for at in (0, node_pad):
            gram[at : at + node_count, :node_count] = high
            gram[at : at + node_count, node_pad : node_pad + node_count] = low
        nodes = jnp.concatenate([nodes_in[0, 0], jnp.full((elements, node_pad - node_count), -1, jnp.int32)], axis=1)
        lists_ref[:elements, :] = nodes.astype(f32)
        stiff_ref[...] = jnp.zeros_like(stiff_ref)
        stiff_ref[:, :elements] = jnp.broadcast_to(stiff_in[0], (stiff_ref.shape[0], elements))
        stiff_ref[...] = jnp.transpose(stiff_ref[...])
        first = rows_of(node_pad) < 4

        def both(source, one):
            here = jnp.broadcast_to(source[one : one + 1, :], (SUB, node_pad))
            return jnp.where(first, here, jnp.broadcast_to(source[one + 1 : one + 2, :], (SUB, node_pad)))

        for one in range(0, elements, 2):
            at = slice(one // 2 * SUB, (one // 2 + 1) * SUB)
            nodes_ref[at, :] = jnp.maximum(both(lists_ref, one), 0.0).astype(jnp.int32)
            scale_ref[at, :] = both(stiff_ref, one)
        columns = jnp.transpose(lists_ref[...]).astype(bf16)
        for one in range(elements):
            b, e = divmod(one, block_elements)
            e_back[b, e * node_pad : (e + 1) * node_pad, :] = spread_columns(columns, one)
        for i in range(others * pairs // LANES):
            c_back[i * LANES : (i + 1) * LANES, :] = spread_columns(columns, contact_row + i)
        for i in range(2 * ghosts // LANES):
            g_back[i * LANES : (i + 1) * LANES, :] = spread_columns(columns, ghost_row + i)

    last = segments - 1
    pl.semaphore_wait(
        barrier, others + lax.div(seg + last, segments) + lax.div(last - seg + last, segments)
    )

    row_all = lax.broadcasted_iota(jnp.int32, (rows, wide), 0) & (SUB - 1)
    low_all = row_all < 4

    def split(x):
        high = x.astype(bf16).astype(f32)
        return jnp.where(low_all, high, x - high).astype(bf16)

    def take(packed, hot, base_ref, start, width):
        cols = slice(start, start + width)
        picked = dot(packed, hot[start // width])
        which = base_ref[:, cols]
        total = jnp.zeros((SUB, width), f32)
        for b in range(blocks):
            total = jnp.where(which == b, picked[b * SUB : (b + 1) * SUB], total)
        return total + pltpu.roll(total, 4, 0)

    def put(values, back, base_ref, start, width):
        cols = slice(start, start + width)
        high = values.astype(bf16).astype(f32)
        values = jnp.where(rows_of(width) < 4, high, values - high)
        which = base_ref[:, cols]
        spread = jnp.concatenate([jnp.where(which == b, values, 0.0) for b in range(blocks)], axis=0)
        return dot(spread.astype(bf16), back[cols, :])

    def take_list(packed, hot, base_ref, start, count, out_ref):
        half = count // 2
        width = hot.shape[2]
        for at in range(0, half, width):
            first = take(packed, hot, base_ref, start + at, width)
            second = take(packed, hot, base_ref, start + half + at, width)
            out_ref[:, at : at + width] = jnp.where(rows_of(width) < 4, first, second)

    def put_list(values, back, base_ref, start, count, width, total):
        half = count // 2
        for at in range(0, half, width):
            here = values[:, at : at + width]
            turned = pltpu.roll(here, 4, 0)
            low = rows_of(width) < 4
            total = total + put(jnp.where(low, here, turned), back, base_ref, start + at, width)
            total = total + put(jnp.where(low, turned, here), back, base_ref, start + half + at, width)
        return total

    def contact_copy(step, d):
        return pltpu.make_async_remote_copy(
            src_ref=c_send.at[d],
            dst_ref=c_recv.at[step, landing(d)],
            send_sem=c_ssem.at[d],
            recv_sem=c_rsem.at[step, landing(d)],
            device_id={"wire": partner(d)},
            device_id_type=MESH,
        )

    def contact_arrival(step, d):
        return pltpu.make_async_remote_copy(
            src_ref=c_send.at[d],
            dst_ref=c_recv.at[step, d],
            send_sem=c_ssem.at[d],
            recv_sem=c_rsem.at[step, d],
            device_id={"wire": partner(d)},
            device_id_type=MESH,
        )

    def ghost_copy(step, side):
        return pltpu.make_async_remote_copy(
            src_ref=g_send.at[side],
            dst_ref=g_recv.at[step, 1 - side],
            send_sem=g_ssem.at[side],
            recv_sem=g_rsem.at[step, 1 - side],
            device_id={"len": seg - 1 if side == 0 else seg + 1},
            device_id_type=MESH,
        )

    def ghost_arrival(step, side):
        return pltpu.make_async_remote_copy(
            src_ref=g_send.at[side],
            dst_ref=g_recv.at[step, side],
            send_sem=g_ssem.at[side],
            recv_sem=g_rsem.at[step, side],
            device_id={"len": seg - 1 if side == 0 else seg + 1},
            device_id_type=MESH,
        )

    exists = (has_prev, has_next)

    def one_step(step, _):
        packed = split(u_ref[...])
        for d in range(others):
            take_list(packed, c_hot, cb_ref, d * pairs, pairs, c_send.at[d])
            contact_copy(step, d).start()

        @pl.when(step == 0)
        def _():
            prepare()

        for b in range(blocks):
            near, far = u_ref[b * SUB : (b + 1) * SUB, :LANES], u_ref[b * SUB : (b + 1) * SUB, LANES:]
            values = []
            for one in (2 * b, 2 * b + 1):
                slots = nodes_ref[one * SUB : (one + 1) * SUB, :]
                inside = slots & (LANES - 1)
                values.append(jnp.where(slots < LANES, lane_take(near, inside), lane_take(far, inside)))
            values = jnp.concatenate(values, axis=0)
            high = values.astype(bf16)
            at = slice(b * 2 * SUB, (b + 1) * 2 * SUB)
            field[at, :node_pad] = high
            field[at, node_pad:] = (values - high.astype(f32)).astype(bf16)
        reach = blocks * 2 * SUB // 4
        first16 = (lax.broadcasted_iota(jnp.int32, (2 * SUB, node_pad), 0) & (SUB - 1)) < 4
        for at in range(0, blocks * 2 * SUB, reach):
            out = dot(field[at : at + reach, :], gram[...])
            out = (out[:, :node_pad] + out[:, node_pad:]) * scale_ref[at : at + reach, :]
            for i in range(0, reach, 2 * SUB):
                b = (at + i) // (2 * SUB)
                pieces = []
                for j in range(2):
                    r = out[i + j * SUB : i + (j + 1) * SUB]
                    high = r.astype(bf16).astype(f32)
                    r = jnp.concatenate([high, r - high], axis=0)
                    pieces.append(jnp.where(first16, r, 0.0).astype(bf16))
                    pieces.append(jnp.where(first16, 0.0, r).astype(bf16))
                here = dot(jnp.concatenate(pieces, axis=1), e_back[b])
                part[b * SUB : (b + 1) * SUB, :] = doubled(here[:SUB] + here[SUB:])

        spread = jnp.zeros((rows, wide), f32)
        for d in reversed(range(others)):
            contact_arrival(step, d).wait_recv()
            spread = put_list(c_recv[step, d] - c_send[d], c_back, cb_ref, d * pairs, pairs, c_hot.shape[2], spread)
        inner = (rows_of(wide) & 3) < 3
        for b in range(blocks):
            at = slice(b * SUB, (b + 1) * SUB)
            part[at, :] = jnp.where(inner, PENALTY * doubled(spread[at]) - part[at, :], mass_ref[at, :])

        packed = split(part[...])
        for side in range(2):
            take_list(packed, g_hot, gb_ref, side * ghosts, ghosts, g_send.at[side])

            @pl.when(exists[side])
            def _():
                ghost_copy(step, side).start()

        spread = jnp.zeros((rows, wide), f32)
        for side in range(2):

            @pl.when(exists[side])
            def _():
                ghost_arrival(step, side).wait_recv()

            spread = put_list(g_recv[step, side], g_back, gb_ref, side * ghosts, ghosts, g_hot.shape[2], spread)
        for b in range(blocks):
            at = slice(b * SUB, (b + 1) * SUB)
            part[at, :] = part[at, :] + doubled(spread[at])

        @pl.when(step == 0)
        def _():
            for b in range(blocks):
                mass = jnp.broadcast_to(part[b * SUB + 3 : b * SUB + 4, :], (SUB, wide))
                rate_ref[b * SUB : (b + 1) * SUB, :] = jnp.where(inner, TIME_SQUARE / mass, 0.0)

        now = u_ref[...]
        u_ref[...] = 2.0 * now - p_ref[...] + rate_ref[...] * part[...]
        p_ref[...] = now

        for d in range(others):
            contact_copy(step, d).wait_send()
        for side in range(2):

            @pl.when(exists[side])
            def _():
                ghost_copy(step, side).wait_send()

        return 0

    lax.fori_loop(0, ITERS, one_step, 0)
    for b in range(blocks):
        lanes = slice(b * block_slots, (b + 1) * block_slots)
        for c in range(parts):
            row = slice(b * SUB + c, b * SUB + c + 1)
            u_out[0, c, :, lanes] = u_ref[row, :block_slots]
            p_out[0, c, :, lanes] = p_ref[row, :block_slots]


def on_device(displacement, previous, element_nodes, *rest):
    left_ghost, contact_slots = rest[3], rest[5]
    node_count, elements = element_nodes.shape[2:]
    blocks = elements // block_elements
    wide = round_up(block_slots, 2 * LANES)
    node_pad = round_up(node_count, LANES)
    wires = lax.axis_size("wire")
    others = wires - 1
    rows = blocks * SUB
    pairs = contact_slots.shape[3]
    ghosts = left_ghost.shape[2]
    c_width, g_width = (512 if x % 512 == 0 else x for x in (pairs // 2, ghosts // 2))
    assert block_elements == 4 and node_pad == LANES and wide == 2 * LANES and blocks % 4 == 0
    assert elements + others * pairs // LANES + 2 * ghosts // LANES <= LANES
    assert all((x * BLOCK_SCALE) >> BLOCK_SHIFT == x // block_slots for x in range(blocks * block_slots))

    vmem = pl.BlockSpec(memory_space=pltpu.VMEM)
    turned = jnp.swapaxes(displacement, 1, 2)
    args = (turned, jnp.swapaxes(previous, 1, 2), jnp.swapaxes(element_nodes, 2, 3), *rest)
    results = pl.pallas_call(
        functools.partial(step_kernel, wires, lax.axis_size("len"), 512),
        out_shape=[jax.ShapeDtypeStruct(turned.shape, f32)] * 2,
        in_specs=[pl.BlockSpec(memory_space=pl.ANY)] * len(args),
        out_specs=[vmem] * 2,
        scratch_shapes=[pltpu.VMEM(x.shape, x.dtype) for x in args]
        + [pltpu.SemaphoreType.DMA((len(args),))]
        + [
            pltpu.VMEM((rows, wide), f32),
            pltpu.VMEM((rows, wide), f32),
            pltpu.VMEM((rows, wide), f32),
            pltpu.VMEM((rows, wide), f32),
            pltpu.VMEM((others * pairs // c_width, wide, c_width), bf16),
            pltpu.VMEM((2 * ghosts // g_width, wide, g_width), bf16),
            pltpu.VMEM((others * pairs, wide), bf16),
            pltpu.VMEM((2 * ghosts, wide), bf16),
            pltpu.VMEM((blocks, block_elements * node_pad, wide), bf16),
            pltpu.VMEM((SUB, others * pairs), jnp.int32),
            pltpu.VMEM((SUB, 2 * ghosts), jnp.int32),
            pltpu.VMEM((2 * node_pad, 2 * node_pad), bf16),
            pltpu.VMEM((elements // 2 * SUB, node_pad), jnp.int32),
            pltpu.VMEM((LANES, LANES), f32),
            pltpu.VMEM((LANES, LANES), f32),
            pltpu.VMEM((elements // 2 * SUB, node_pad), f32),
            pltpu.VMEM((rows, wide), f32),
            pltpu.VMEM((elements // 2 * SUB, 2 * node_pad), bf16),
            pltpu.VMEM((others, SUB, pairs // 2), f32),
            pltpu.VMEM((ITERS, others, SUB, pairs // 2), f32),
            pltpu.VMEM((2, SUB, ghosts // 2), f32),
            pltpu.VMEM((ITERS, 2, SUB, ghosts // 2), f32),
            pltpu.SemaphoreType.DMA((others,)),
            pltpu.SemaphoreType.DMA((ITERS, others)),
            pltpu.SemaphoreType.DMA((2,)),
            pltpu.SemaphoreType.DMA((ITERS, 2)),
        ],
        compiler_params=pltpu.CompilerParams(
            collective_id=0, has_side_effects=True, vmem_limit_bytes=VMEM_BYTES
        ),
        name="steps",
    )(*args)
    return tuple(jnp.swapaxes(x, 1, 2) for x in results)


def solution(mesh):
    four = P("len", "wire", None, None)
    three = P("len", "wire", None)
    return jax.shard_map(
        on_device,
        mesh=mesh,
        in_specs=(four, four, four, three, P(), three, three, three, four, four),
        out_specs=(four, four),
        check_vma=False,
    )
```

```python
import functools

import jax
import jax.numpy as jnp
from jax import lax
from jax.experimental import pallas as pl
from jax.experimental.pallas import tpu as pltpu
from jax.sharding import PartitionSpec as P

ITERS = 4
PENALTY = 4.0
TIME_SQUARE = 0.03
block_slots = 224
block_elements = 4
LANES = 128
ARGS = 10
VMEM_BYTES = 67_043_328
FIRST = (6, 7, 8, 9, 0)
LATER = (1, 2, 3, 4, 5)
BLOCK_SCALE, BLOCK_SHIFT = 4682, 20
SUB = 8
f32 = jnp.float32
bf16 = jnp.bfloat16
MESH = pl.DeviceIdType.MESH


def round_up(value, step):
    return -(-value // step) * step


def dot(a, b):
    return jnp.dot(a, b, preferred_element_type=f32)


def dot_nt(a, b):
    return lax.dot_general(a, b, (((1,), (1,)), ((), ())), preferred_element_type=f32)


def lane_take(values, lanes):
    return jnp.take_along_axis(values, lanes, axis=1, mode="promise_in_bounds")


def step_kernel(
    wires,
    segments,
    chunk,
    *refs,
):
    sources, refs = refs[:ARGS], refs[ARGS:]
    inputs, in_sem, refs = refs[2 : 2 + ARGS], refs[2 + ARGS], refs[:2] + refs[3 + ARGS :]
    copies = [
        pltpu.make_async_copy(source, target, in_sem.at[i])
        for i, (source, target) in enumerate(zip(sources, inputs))
    ]
    for i in FIRST + LATER:
        copies[i].start()
    run(wires, segments, chunk, copies, *inputs, *refs)


def run(
    wires,
    segments,
    chunk,
    copies,
    u_in, p_in, nodes_in, stiff_in, grad_in, mass_in, left_in, right_in, slots_in, live_in,
    u_out, p_out,
    u_ref, p_ref, mass_ref, rate_ref,
    c_hot, g_hot, c_back, g_back, x_back, e_back, cb_ref, gb_ref, xb_ref, count_ref, gram, nodes_ref, lists_ref, stiff_ref, scale_ref,
    part, field, c_send, c_recv, g_send, g_recv, x_send, x_recv,
    c_ssem, c_rsem, g_ssem, g_rsem, x_ssem, x_rsem,
):
    others = wires - 1
    direct = x_send.shape[0]
    blocks = e_back.shape[0]
    parts = u_in.shape[1]
    rows, wide = u_ref.shape
    pairs = slots_in.shape[3]
    ghosts = left_in.shape[2]
    elements, node_count = nodes_in.shape[2:]
    node_pad = gram.shape[0] // 2
    contact_row = elements
    ghost_row = contact_row + others * pairs // LANES
    me = lax.axis_index("wire")
    seg = lax.axis_index("len")
    has_prev = seg > 0
    has_next = seg < segments - 1
    half = ghosts // 2
    full, rest = divmod(half, wide)
    places = [(h * half + i * wide, wide, 2 * i + h, 0) for i in range(full) for h in range(2)]
    places += [(h * half + full * wide, rest, 2 * full, h * LANES) for h in range(2) if rest]
    groups = 2 * full + (rest > 0)
    mirrored = wires & (wires - 1) == 0

    def partner(d):
        if not mirrored:
            return lax.rem(me + (d + 1), wires)
        offset, other, bit = wires - 1 - d, me, 1
        while bit <= offset:
            if offset & bit:
                other = other + bit - 2 * bit * lax.rem(lax.div(me, bit), 2)
            bit *= 2
        return other

    def landing(d):
        return d if mirrored else others - 1 - d

    barrier = pltpu.get_barrier_semaphore()
    for d in range(others):
        pl.semaphore_signal(barrier, inc=1, device_id={"wire": partner(d)}, device_id_type=MESH)

    @pl.when(has_prev)
    def _():
        pl.semaphore_signal(barrier, inc=1, device_id={"len": seg - 1}, device_id_type=MESH)
        for d in range(direct):
            there = {"len": seg - 1, "wire": partner(d)}
            pl.semaphore_signal(barrier, inc=1, device_id=there, device_id_type=MESH)

    @pl.when(has_next)
    def _():
        pl.semaphore_signal(barrier, inc=1, device_id={"len": seg + 1}, device_id_type=MESH)
        for d in range(direct):
            there = {"len": seg + 1, "wire": partner(d)}
            pl.semaphore_signal(barrier, inc=1, device_id=there, device_id_type=MESH)

    def rows_of(width):
        return lax.broadcasted_iota(jnp.int32, (SUB, width), 0)

    def doubled(x):
        return x + pltpu.roll(x, 4, 0)

    def placed(values, base_ref, start, width, parts):
        high = values.astype(bf16).astype(f32)
        values = jnp.where(rows_of(width) < 4, high, values - high)
        which = base_ref[:, start : start + width]
        return jnp.concatenate([jnp.where(which == b, values, 0.0) for b in range(parts)], axis=0).astype(bf16)

    def put(values, back, base_ref, start, width, parts):
        return dot(placed(values, base_ref, start, width, parts), back[start : start + width, :])

    def match(slots):
        ids = lax.broadcasted_iota(jnp.int32, (wide, LANES), 0).astype(bf16)
        here = jnp.broadcast_to(slots.astype(f32), (2 * SUB, LANES)).astype(bf16)
        here = jnp.concatenate([here] * (wide // (2 * SUB)), axis=0)
        return jnp.where(ids == here, jnp.ones((), bf16), jnp.zeros((), bf16))

    def block_of(slots):
        return (slots * BLOCK_SCALE) >> BLOCK_SHIFT

    def spread_columns(columns, at):
        lanes = lax.broadcasted_iota(jnp.int32, (LANES, wide), 1).astype(bf16)
        here = jnp.broadcast_to(columns[:, at : at + 1], (LANES, wide))
        return jnp.where(lanes == here, jnp.ones((), bf16), jnp.zeros((), bf16))

    def fill(hot, base_ref, at, slots, live, row):
        count = slots.shape[1]
        which = block_of(slots)
        inside = slots - which * block_slots
        if live is not None:
            which = jnp.where(live > 0, which, -1)
        base_ref[:, at : at + count] = jnp.broadcast_to(which, (SUB, count))
        for start in range(0, count, LANES):
            here = inside[:, start : start + LANES]
            group, lane = divmod(at + start, hot.shape[2])
            hot[group, :, lane : lane + LANES] = match(here)
            at_row = row + (at + start) // LANES
            lists_ref[at_row : at_row + 1, :] = here.astype(f32)

    for i in FIRST:
        copies[i].wait()
    u_ref[...] = jnp.zeros_like(u_ref)
    p_ref[...] = jnp.zeros_like(p_ref)
    lists_ref[...] = jnp.zeros_like(lists_ref)
    for b in range(blocks):
        lanes = slice(b * block_slots, (b + 1) * block_slots)
        for c in range(parts):
            row = slice(b * SUB + c, b * SUB + c + 1)
            u_ref[row, :block_slots] = u_in[0, c, :, lanes]
    fill(g_hot, gb_ref, 0, left_in[0], None, ghost_row)
    fill(g_hot, gb_ref, ghosts, right_in[0], None, ghost_row)
    codes = []
    for side in range(2):
        for _, count, group, at in sorted(places):
            code = lax.broadcasted_iota(jnp.int32, (SUB, count), 1) + (wide * (side * groups + group + 1) + at)
            codes.append(code.astype(f32))
    codes = jnp.concatenate(codes, axis=1)
    last_row = (rows_of(wide) & 3) == 3
    codes = dot_nt(placed(codes, gb_ref, 0, 2 * ghosts, blocks), g_hot[0])
    for b in range(blocks):
        at = slice(b * SUB, (b + 1) * SUB)
        u_ref[at, :] = jnp.where(last_row, doubled(codes[at]), doubled(u_ref[at, :]))
    for d in range(others):
        fill(c_hot, cb_ref, d * pairs, slots_in[0, 0, pl.ds(partner(d), 1), :], live_in[0, 0, pl.ds(partner(d), 1), :], contact_row)

    @pl.when(jnp.logical_not(has_prev))
    def _():
        g_recv[:, 0] = jnp.zeros((ITERS,) + g_recv.shape[2:], f32)
        for d in range(direct):
            x_recv[:, d, 0] = jnp.zeros((ITERS,) + x_recv.shape[3:], f32)

    @pl.when(jnp.logical_not(has_next))
    def _():
        g_recv[:, 1] = jnp.zeros((ITERS,) + g_recv.shape[2:], f32)
        for d in range(direct):
            x_recv[:, d, 1] = jnp.zeros((ITERS,) + x_recv.shape[3:], f32)

    def prepare():
        for i in LATER:
            copies[i].wait()
        mass_ref[...] = jnp.zeros_like(mass_ref)
        for b in range(blocks):
            at = slice(b * SUB, (b + 1) * SUB)
            lanes = slice(b * block_slots, (b + 1) * block_slots)
            for c in range(parts):
                p_ref[b * SUB + c : b * SUB + c + 1, :block_slots] = p_in[0, c, :, lanes]
            p_ref[at, :] = jnp.where((rows_of(wide) & 3) < 3, doubled(p_ref[at, :]), u_ref[at, :])
            mass_ref[b * SUB + 3 : b * SUB + 4, :] = jnp.ones((1, wide), f32)
            mass_ref[b * SUB + 3 : b * SUB + 4, :block_slots] = mass_in[0, :, lanes]
            mass_ref[at, :] = doubled(mass_ref[at, :])
        op = grad_in[...]
        product = lax.dot_general(
            op, op, (((0,), (0,)), ((), ())), precision=lax.Precision.HIGHEST, preferred_element_type=f32
        )
        high = product.astype(bf16)
        low = (product - high.astype(f32)).astype(bf16)
        gram[...] = jnp.zeros_like(gram)
        for at in (0, node_pad):
            gram[at : at + node_count, :node_count] = high
            gram[at : at + node_count, node_pad : node_pad + node_count] = low
        nodes = jnp.concatenate([nodes_in[0, 0], jnp.full((elements, node_pad - node_count), -1, jnp.int32)], axis=1)
        lists_ref[:elements, :] = nodes.astype(f32)
        stiff_ref[...] = jnp.zeros_like(stiff_ref)
        stiff_ref[:, :elements] = jnp.broadcast_to(stiff_in[0], (stiff_ref.shape[0], elements))
        stiff_ref[...] = jnp.transpose(stiff_ref[...])
        first = rows_of(node_pad) < 4

        def both(source, one):
            here = jnp.broadcast_to(source[one : one + 1, :], (SUB, node_pad))
            return jnp.where(first, here, jnp.broadcast_to(source[one + 1 : one + 2, :], (SUB, node_pad)))

        for one in range(0, elements, 2):
            at = slice(one // 2 * SUB, (one // 2 + 1) * SUB)
            nodes_ref[at, :] = jnp.maximum(both(lists_ref, one), 0.0).astype(jnp.int32)
            scale_ref[at, :] = both(stiff_ref, one)
        columns = jnp.transpose(lists_ref[...]).astype(bf16)
        for one in range(elements):
            b, e = divmod(one, block_elements)
            e_back[b, e * node_pad : (e + 1) * node_pad, :] = spread_columns(columns, one)
        for i in range(others * pairs // LANES):
            c_back[i * LANES : (i + 1) * LANES, :] = spread_columns(columns, contact_row + i)
        for i in range(2 * ghosts // LANES):
            g_back[i * LANES : (i + 1) * LANES, :] = spread_columns(columns, ghost_row + i)
        total = jnp.zeros((rows, wide), f32)
        width = c_hot.shape[2]
        for at in range(0, direct * pairs, width):
            total = total + put(jnp.ones((SUB, width), f32), c_back, cb_ref, at, width, blocks)
        for b in range(blocks):
            at = slice(b * SUB, (b + 1) * SUB)
            count_ref[at, :] = jnp.where((rows_of(wide) & 3) < 3, PENALTY * doubled(total[at]), 0.0)

    def prepare_direct():
        for d in range(direct):
            live = live_in[0, 0, pl.ds(partner(d), 1), :]
            for k in range(pairs // LANES):
                h, at = divmod(k * LANES, pairs // 2)
                code = c_recv[0, d, 4 * h + 3 : 4 * h + 4, at : at + LANES]
                group = jnp.floor(code * (1.0 / wide))
                i = d * (pairs // LANES) + k
                lists_ref[i : i + 1, :] = code - wide * group
                alive = live[:, k * LANES : (k + 1) * LANES] > 0
                which = jnp.where(alive, group.astype(jnp.int32) - 1, -1)
                xb_ref[:, i * LANES : (i + 1) * LANES] = jnp.broadcast_to(which, (SUB, LANES))
        columns = jnp.transpose(lists_ref[...]).astype(bf16)
        for i in range(direct * pairs // LANES):
            x_back[i * LANES : (i + 1) * LANES, :] = spread_columns(columns, i)

    last = segments - 1
    pl.semaphore_wait(
        barrier, others + (direct + 1) * (lax.div(seg + last, segments) + lax.div(last - seg + last, segments))
    )

    row_all = lax.broadcasted_iota(jnp.int32, (rows, wide), 0) & (SUB - 1)
    low_all = row_all < 4

    def split(x):
        high = x.astype(bf16).astype(f32)
        return jnp.where(low_all, high, x - high).astype(bf16)

    def take(packed, hot, which):
        width = which.shape[1]
        picked = dot(packed, hot)
        total = jnp.zeros((SUB, width), f32)
        for b in range(blocks):
            total = jnp.where(which == b, picked[b * SUB : (b + 1) * SUB], total)
        return doubled(total)

    def take_list(packed, d, out_ref):
        width = c_hot.shape[2]
        for at in range(0, pairs // 2, width):
            both = []
            for start in (d * pairs + at, d * pairs + pairs // 2 + at):
                both.append(take(packed, c_hot[start // width], cb_ref[:, start : start + width]))
            out_ref[:, at : at + width] = jnp.where(rows_of(width) < 4, *both)

    def halves(here):
        turned = pltpu.roll(here, 4, 0)
        low = rows_of(here.shape[1]) < 4
        return jnp.where(low, here, turned), jnp.where(low, turned, here)

    def put_list(values, back, base_ref, d, parts, total):
        width = c_hot.shape[2]
        for at in range(0, pairs // 2, width):
            for h, here in enumerate(halves(values[:, at : at + width])):
                total = total + put(here, back, base_ref, d * pairs + h * (pairs // 2) + at, width, parts)
        return total

    def contact_copy(step, d):
        return pltpu.make_async_remote_copy(
            src_ref=c_send.at[d],
            dst_ref=c_recv.at[step, landing(d)],
            send_sem=c_ssem.at[d],
            recv_sem=c_rsem.at[step, landing(d)],
            device_id={"wire": partner(d)},
            device_id_type=MESH,
        )

    def contact_arrival(step, d):
        return pltpu.make_async_remote_copy(
            src_ref=c_send.at[d],
            dst_ref=c_recv.at[step, d],
            send_sem=c_ssem.at[d],
            recv_sem=c_rsem.at[step, d],
            device_id={"wire": partner(d)},
            device_id_type=MESH,
        )

    def ghost_copy(step, side):
        return pltpu.make_async_remote_copy(
            src_ref=g_send.at[side],
            dst_ref=g_recv.at[step, 1 - side],
            send_sem=g_ssem.at[side],
            recv_sem=g_rsem.at[step, 1 - side],
            device_id={"len": seg - 1 if side == 0 else seg + 1},
            device_id_type=MESH,
        )

    def ghost_arrival(step, side):
        return pltpu.make_async_remote_copy(
            src_ref=g_send.at[side],
            dst_ref=g_recv.at[step, side],
            send_sem=g_ssem.at[side],
            recv_sem=g_rsem.at[step, side],
            device_id={"len": seg - 1 if side == 0 else seg + 1},
            device_id_type=MESH,
        )

    def direct_copy(step, d, side):
        return pltpu.make_async_remote_copy(
            src_ref=x_send.at[d, side],
            dst_ref=x_recv.at[step, landing(d), 1 - side],
            send_sem=x_ssem.at[d, side],
            recv_sem=x_rsem.at[step, landing(d), 1 - side],
            device_id={"len": seg - 1 if side == 0 else seg + 1, "wire": partner(d)},
            device_id_type=MESH,
        )

    def direct_arrival(step, d, side):
        return pltpu.make_async_remote_copy(
            src_ref=x_send.at[d, side],
            dst_ref=x_recv.at[step, d, side],
            send_sem=x_ssem.at[d, side],
            recv_sem=x_rsem.at[step, d, side],
            device_id={"len": seg - 1 if side == 0 else seg + 1, "wire": partner(d)},
            device_id_type=MESH,
        )

    exists = (has_prev, has_next)

    def one_step(step, first):
        packed = split(u_ref[...])
        for d in range(others):
            take_list(packed, d, c_send.at[d])
        if first:
            for d in range(others):
                contact_copy(step, d).start()
            prepare()
            for d in range(direct):
                contact_arrival(step, d).wait_recv()
            prepare_direct()
        for d in range(direct):
            total = put_list(c_send[d], x_back, xb_ref, d, 2 * groups, jnp.zeros((2 * groups * SUB, wide), f32))
            total = [doubled(total[i * SUB : (i + 1) * SUB]) for i in range(2 * groups)]
            for side in range(2):
                mine = total[side * groups : (side + 1) * groups]
                for i in range(full):
                    x_send[d, side, :, i * wide : (i + 1) * wide] = jnp.where(rows_of(wide) < 4, mine[2 * i], mine[2 * i + 1])
                if rest:
                    shared = jnp.where(rows_of(LANES) < 4, mine[2 * full][:, :LANES], mine[2 * full][:, LANES:])
                    x_send[d, side, :, full * wide :] = shared
        for side in range(2):

            @pl.when(exists[side])
            def _():
                for d in range(direct):
                    direct_copy(step, d, side).start()

        if not first:
            for d in reversed(range(others)):
                contact_copy(step, d).start()

        for b in range(blocks):
            near, far = u_ref[b * SUB : (b + 1) * SUB, :LANES], u_ref[b * SUB : (b + 1) * SUB, LANES:]
            values = []
            for one in (2 * b, 2 * b + 1):
                slots = nodes_ref[one * SUB : (one + 1) * SUB, :]
                inside = slots & (LANES - 1)
                values.append(jnp.where(slots < LANES, lane_take(near, inside), lane_take(far, inside)))
            values = jnp.concatenate(values, axis=0)
            high = values.astype(bf16)
            at = slice(b * 2 * SUB, (b + 1) * 2 * SUB)
            field[at, :node_pad] = high
            field[at, node_pad:] = (values - high.astype(f32)).astype(bf16)
        reach = blocks * 2 * SUB // 4
        first16 = (lax.broadcasted_iota(jnp.int32, (2 * SUB, node_pad), 0) & (SUB - 1)) < 4
        for at in range(0, blocks * 2 * SUB, reach):
            out = dot(field[at : at + reach, :], gram[...])
            out = (out[:, :node_pad] + out[:, node_pad:]) * scale_ref[at : at + reach, :]
            for i in range(0, reach, 2 * SUB):
                b = (at + i) // (2 * SUB)
                pieces = []
                for j in range(2):
                    r = out[i + j * SUB : i + (j + 1) * SUB]
                    high = r.astype(bf16).astype(f32)
                    r = jnp.concatenate([high, r - high], axis=0)
                    pieces.append(jnp.where(first16, r, 0.0).astype(bf16))
                    pieces.append(jnp.where(first16, 0.0, r).astype(bf16))
                here = dot(jnp.concatenate(pieces, axis=1), e_back[b])
                part[b * SUB : (b + 1) * SUB, :] = doubled(here[:SUB] + here[SUB:])

        spread = jnp.zeros((rows, wide), f32)
        for d in range(direct, others):
            contact_arrival(step, d).wait_recv()
            spread = put_list(c_recv[step, d] - c_send[d], c_back, cb_ref, d, blocks, spread)
        inner = (rows_of(wide) & 3) < 3
        for b in range(blocks):
            at = slice(b * SUB, (b + 1) * SUB)
            own = PENALTY * doubled(spread[at]) - part[at, :] - count_ref[at, :] * u_ref[at, :]
            part[at, :] = jnp.where(inner, own, mass_ref[at, :])

        picked = take(split(part[...]), g_hot[0], gb_ref[...])
        for side in range(2):
            at = side * ghosts
            g_send[side] = jnp.where(rows_of(half) < 4, picked[:, at : at + half], picked[:, at + half : at + ghosts])
        for side in range(2):

            @pl.when(exists[side])
            def _():
                ghost_copy(step, side).start()

        spread = jnp.zeros((rows, wide), f32)
        for d in range(direct):
            if not first:
                contact_arrival(step, d).wait_recv()
            spread = put_list(c_recv[step, d], c_back, cb_ref, d, blocks, spread)
        for b in range(blocks):
            at = slice(b * SUB, (b + 1) * SUB)
            part[at, :] = part[at, :] + jnp.where(inner, PENALTY * doubled(spread[at]), 0.0)

        for side in range(2):

            @pl.when(exists[side])
            def _():
                ghost_arrival(step, side).wait_recv()
                for d in range(direct):
                    direct_arrival(step, d, side).wait_recv()

        arrived = []
        for side in range(2):
            crossed = sum(x_recv[step, d, side] for d in range(direct))
            crossed = jnp.where((rows_of(half) & 3) < 3, PENALTY * crossed, 0.0)
            arrived += halves(g_recv[step, side] + crossed)
        spread = put(jnp.concatenate(arrived, axis=1), g_back, gb_ref, 0, 2 * ghosts, blocks)
        for b in range(blocks):
            at = slice(b * SUB, (b + 1) * SUB)
            part[at, :] = part[at, :] + doubled(spread[at])

        if first:
            for b in range(blocks):
                mass = jnp.broadcast_to(part[b * SUB + 3 : b * SUB + 4, :], (SUB, wide))
                rate_ref[b * SUB : (b + 1) * SUB, :] = jnp.where(inner, TIME_SQUARE / mass, 0.0)

        now = u_ref[...]
        u_ref[...] = 2.0 * now - p_ref[...] + rate_ref[...] * part[...]
        p_ref[...] = now

        for d in range(others):
            contact_copy(step, d).wait_send()
        for side in range(2):

            @pl.when(exists[side])
            def _():
                ghost_copy(step, side).wait_send()
                for d in range(direct):
                    direct_copy(step, d, side).wait_send()

    one_step(0, True)

    def later_step(step, _):
        one_step(step, False)
        return 0

    lax.fori_loop(1, ITERS, later_step, 0)
    for b in range(blocks):
        lanes = slice(b * block_slots, (b + 1) * block_slots)
        for c in range(parts):
            row = slice(b * SUB + c, b * SUB + c + 1)
            u_out[0, c, :, lanes] = u_ref[row, :block_slots]
            p_out[0, c, :, lanes] = p_ref[row, :block_slots]


def hand_on(u_from, p_from, u_to, p_to):
    u_to[...] = u_from[...]
    p_to[...] = p_from[...]


def on_device(displacement, previous, element_nodes, *rest):
    left_ghost, contact_slots = rest[3], rest[5]
    node_count, elements = element_nodes.shape[2:]
    blocks = elements // block_elements
    wide = round_up(block_slots, 2 * LANES)
    node_pad = round_up(node_count, LANES)
    wires = lax.axis_size("wire")
    others = wires - 1
    rows = blocks * SUB
    pairs = contact_slots.shape[3]
    ghosts = left_ghost.shape[2]
    c_width = 512 if pairs % 1024 == 0 else pairs // 2
    mirrored = wires & (wires - 1) == 0
    direct = others - 1 if mirrored else others
    groups = 2 * (ghosts // 2 // wide) + (ghosts // 2 % wide > 0)
    assert block_elements == 4 and node_pad == LANES and wide == 2 * LANES and blocks % 4 == 0
    assert elements + others * pairs // LANES + 2 * ghosts // LANES <= LANES
    assert direct > 0 and ghosts // 2 % wide in (0, LANES) and direct * pairs <= LANES * LANES
    assert wide * (2 * groups + 1) < 65536
    assert all((x * BLOCK_SCALE) >> BLOCK_SHIFT == x // block_slots for x in range(blocks * block_slots))

    vmem = pl.BlockSpec(memory_space=pltpu.VMEM)
    turned = jnp.swapaxes(displacement, 1, 2)
    args = (turned, jnp.swapaxes(previous, 1, 2), jnp.swapaxes(element_nodes, 2, 3), *rest)
    results = pl.pallas_call(
        functools.partial(step_kernel, wires, lax.axis_size("len"), 512),
        out_shape=[jax.ShapeDtypeStruct(turned.shape, f32)] * 2,
        in_specs=[pl.BlockSpec(memory_space=pl.ANY)] * len(args),
        out_specs=[vmem] * 2,
        scratch_shapes=[pltpu.VMEM(x.shape, x.dtype) for x in args]
        + [pltpu.SemaphoreType.DMA((len(args),))]
        + [
            pltpu.VMEM((rows, wide), f32),
            pltpu.VMEM((rows, wide), f32),
            pltpu.VMEM((rows, wide), f32),
            pltpu.VMEM((rows, wide), f32),
            pltpu.VMEM((others * pairs // c_width, wide, c_width), bf16),
            pltpu.VMEM((1, wide, 2 * ghosts), bf16),
            pltpu.VMEM((others * pairs, wide), bf16),
            pltpu.VMEM((2 * ghosts, wide), bf16),
            pltpu.VMEM((direct * pairs, wide), bf16),
            pltpu.VMEM((blocks, block_elements * node_pad, wide), bf16),
            pltpu.VMEM((SUB, others * pairs), jnp.int32),
            pltpu.VMEM((SUB, 2 * ghosts), jnp.int32),
            pltpu.VMEM((SUB, direct * pairs), jnp.int32),
            pltpu.VMEM((rows, wide), f32),
            pltpu.VMEM((2 * node_pad, 2 * node_pad), bf16),
            pltpu.VMEM((elements // 2 * SUB, node_pad), jnp.int32),
            pltpu.VMEM((LANES, LANES), f32),
            pltpu.VMEM((LANES, LANES), f32),
            pltpu.VMEM((elements // 2 * SUB, node_pad), f32),
            pltpu.VMEM((rows, wide), f32),
            pltpu.VMEM((elements // 2 * SUB, 2 * node_pad), bf16),
            pltpu.VMEM((others, SUB, pairs // 2), f32),
            pltpu.VMEM((ITERS, others, SUB, pairs // 2), f32),
            pltpu.VMEM((2, SUB, ghosts // 2), f32),
            pltpu.VMEM((ITERS, 2, SUB, ghosts // 2), f32),
            pltpu.VMEM((direct, 2, SUB, ghosts // 2), f32),
            pltpu.VMEM((ITERS, direct, 2, SUB, ghosts // 2), f32),
            pltpu.SemaphoreType.DMA((others,)),
            pltpu.SemaphoreType.DMA((ITERS, others)),
            pltpu.SemaphoreType.DMA((2,)),
            pltpu.SemaphoreType.DMA((ITERS, 2)),
            pltpu.SemaphoreType.DMA((direct, 2)),
            pltpu.SemaphoreType.DMA((ITERS, direct, 2)),
        ],
        compiler_params=pltpu.CompilerParams(
            collective_id=0, has_side_effects=True, vmem_limit_bytes=VMEM_BYTES
        ),
        name="steps",
    )(*args)
    results = pl.pallas_call(
        hand_on,
        out_shape=[jax.ShapeDtypeStruct(turned.shape, f32)] * 2,
        in_specs=[vmem] * 2,
        out_specs=[vmem] * 2,
        name="hand_on",
    )(*results)
    return tuple(jnp.swapaxes(x, 1, 2) for x in results)


def solution(mesh):
    four = P("len", "wire", None, None)
    three = P("len", "wire", None)
    return jax.shard_map(
        on_device,
        mesh=mesh,
        in_specs=(four, four, four, three, P(), three, three, three, four, four),
        out_specs=(four, four),
        check_vma=False,
    )
```

```python
import functools

import jax
import jax.numpy as jnp
from jax import lax
from jax.experimental import pallas as pl
from jax.experimental.pallas import tpu as pltpu
from jax.sharding import PartitionSpec as P

ITERS = 4
PENALTY = 4.0
TIME_SQUARE = 0.03
block_slots = 224
block_elements = 4
LANES = 128
ARGS = 10
VMEM_BYTES = 67_043_328
FIRST = (6, 7, 8, 9, 0)
LATER = (1, 2, 3, 4, 5)
BLOCK_SCALE, BLOCK_SHIFT = 4682, 20
SUB = 8
f32 = jnp.float32
bf16 = jnp.bfloat16
MESH = pl.DeviceIdType.MESH


def round_up(value, step):
    return -(-value // step) * step


def dot(a, b):
    return jnp.dot(a, b, preferred_element_type=f32)


def dot_nt(a, b):
    return lax.dot_general(a, b, (((1,), (1,)), ((), ())), preferred_element_type=f32)


def lane_take(values, lanes):
    return jnp.take_along_axis(values, lanes, axis=1, mode="promise_in_bounds")


def step_kernel(
    wires,
    segments,
    chunk,
    *refs,
):
    sources, refs = refs[:ARGS], refs[ARGS:]
    inputs, in_sem, refs = refs[2 : 2 + ARGS], refs[2 + ARGS], refs[:2] + refs[3 + ARGS :]
    copies = [
        pltpu.make_async_copy(source, target, in_sem.at[i])
        for i, (source, target) in enumerate(zip(sources, inputs))
    ]
    for i in FIRST + LATER:
        copies[i].start()
    run(wires, segments, chunk, copies, *inputs, *refs)


def run(
    wires,
    segments,
    chunk,
    copies,
    u_in, p_in, nodes_in, stiff_in, grad_in, mass_in, left_in, right_in, slots_in, live_in,
    u_out, p_out,
    u_ref, p_ref, mass_ref, rate_ref,
    c_hot, g_hot, c_back, g_back, x_back, e_back, cb_ref, gb_ref, xb_ref, count_ref, gram, nodes_ref, lists_ref, stiff_ref, scale_ref,
    part, field, pushed, c_send, c_recv, g_send, g_recv, x_send, x_recv,
    c_ssem, c_rsem, g_ssem, g_rsem, x_ssem, x_rsem,
):
    others = wires - 1
    direct = x_send.shape[0]
    blocks = e_back.shape[0]
    parts = u_in.shape[1]
    rows, wide = u_ref.shape
    pairs = slots_in.shape[3]
    ghosts = left_in.shape[2]
    elements, node_count = nodes_in.shape[2:]
    node_pad = gram.shape[0] // 2
    contact_row = elements
    ghost_row = contact_row + others * pairs // LANES
    me = lax.axis_index("wire")
    seg = lax.axis_index("len")
    has_prev = seg > 0
    has_next = seg < segments - 1
    half = ghosts // 2
    full, rest = divmod(half, wide)
    places = [(h * half + i * wide, wide, 2 * i + h, 0) for i in range(full) for h in range(2)]
    places += [(h * half + full * wide, rest, 2 * full, h * LANES) for h in range(2) if rest]
    groups = 2 * full + (rest > 0)
    mirrored = wires & (wires - 1) == 0

    def partner(d):
        if not mirrored:
            return lax.rem(me + (d + 1), wires)
        offset, other, bit = wires - 1 - d, me, 1
        while bit <= offset:
            if offset & bit:
                other = other + bit - 2 * bit * lax.rem(lax.div(me, bit), 2)
            bit *= 2
        return other

    def landing(d):
        return d if mirrored else others - 1 - d

    barrier = pltpu.get_barrier_semaphore()
    for d in range(others):
        pl.semaphore_signal(barrier, inc=1, device_id={"wire": partner(d)}, device_id_type=MESH)

    @pl.when(has_prev)
    def _():
        pl.semaphore_signal(barrier, inc=1, device_id={"len": seg - 1}, device_id_type=MESH)
        for d in range(direct):
            there = {"len": seg - 1, "wire": partner(d)}
            pl.semaphore_signal(barrier, inc=1, device_id=there, device_id_type=MESH)

    @pl.when(has_next)
    def _():
        pl.semaphore_signal(barrier, inc=1, device_id={"len": seg + 1}, device_id_type=MESH)
        for d in range(direct):
            there = {"len": seg + 1, "wire": partner(d)}
            pl.semaphore_signal(barrier, inc=1, device_id=there, device_id_type=MESH)

    def rows_of(width):
        return lax.broadcasted_iota(jnp.int32, (SUB, width), 0)

    def doubled(x):
        return x + pltpu.roll(x, 4, 0)

    def placed(values, base_ref, start, width, parts):
        high = values.astype(bf16).astype(f32)
        values = jnp.where(rows_of(width) < 4, high, values - high)
        which = base_ref[:, start : start + width]
        return jnp.concatenate([jnp.where(which == b, values, 0.0) for b in range(parts)], axis=0).astype(bf16)

    def put(values, back, base_ref, start, width, parts):
        return dot(placed(values, base_ref, start, width, parts), back[start : start + width, :])

    def match(slots):
        ids = lax.broadcasted_iota(jnp.int32, (wide, LANES), 0).astype(bf16)
        here = jnp.broadcast_to(slots.astype(f32), (2 * SUB, LANES)).astype(bf16)
        here = jnp.concatenate([here] * (wide // (2 * SUB)), axis=0)
        return jnp.where(ids == here, jnp.ones((), bf16), jnp.zeros((), bf16))

    def block_of(slots):
        return (slots * BLOCK_SCALE) >> BLOCK_SHIFT

    def spread_columns(columns, at):
        lanes = lax.broadcasted_iota(jnp.int32, (LANES, wide), 1).astype(bf16)
        here = jnp.broadcast_to(columns[:, at : at + 1], (LANES, wide))
        return jnp.where(lanes == here, jnp.ones((), bf16), jnp.zeros((), bf16))

    def fill(hot, base_ref, at, slots, live, row):
        count = slots.shape[1]
        which = block_of(slots)
        inside = slots - which * block_slots
        if live is not None:
            which = jnp.where(live > 0, which, -1)
        base_ref[:, at : at + count] = jnp.broadcast_to(which, (SUB, count))
        for start in range(0, count, LANES):
            here = inside[:, start : start + LANES]
            group, lane = divmod(at + start, hot.shape[2])
            hot[group, :, lane : lane + LANES] = match(here)
            at_row = row + (at + start) // LANES
            lists_ref[at_row : at_row + 1, :] = here.astype(f32)

    for i in FIRST:
        copies[i].wait()
    u_ref[...] = jnp.zeros_like(u_ref)
    p_ref[...] = jnp.zeros_like(p_ref)
    lists_ref[...] = jnp.zeros_like(lists_ref)
    for b in range(blocks):
        lanes = slice(b * block_slots, (b + 1) * block_slots)
        for c in range(parts):
            row = slice(b * SUB + c, b * SUB + c + 1)
            u_ref[row, :block_slots] = u_in[0, c, :, lanes]
    fill(g_hot, gb_ref, 0, left_in[0], None, ghost_row)
    fill(g_hot, gb_ref, ghosts, right_in[0], None, ghost_row)
    codes = []
    for side in range(2):
        for _, count, group, at in sorted(places):
            code = lax.broadcasted_iota(jnp.int32, (SUB, count), 1) + (wide * (side * groups + group + 1) + at)
            codes.append(code.astype(f32))
    codes = jnp.concatenate(codes, axis=1)
    last_row = (rows_of(wide) & 3) == 3
    codes = dot_nt(placed(codes, gb_ref, 0, 2 * ghosts, blocks), g_hot[0])
    for b in range(blocks):
        at = slice(b * SUB, (b + 1) * SUB)
        u_ref[at, :] = jnp.where(last_row, doubled(codes[at]), doubled(u_ref[at, :]))
    for d in range(others):
        fill(c_hot, cb_ref, d * pairs, slots_in[0, 0, pl.ds(partner(d), 1), :], live_in[0, 0, pl.ds(partner(d), 1), :], contact_row)

    @pl.when(jnp.logical_not(has_prev))
    def _():
        g_recv[:, 0] = jnp.zeros((ITERS,) + g_recv.shape[2:], f32)
        for d in range(direct):
            x_recv[:, d, 0] = jnp.zeros((ITERS,) + x_recv.shape[3:], f32)

    @pl.when(jnp.logical_not(has_next))
    def _():
        g_recv[:, 1] = jnp.zeros((ITERS,) + g_recv.shape[2:], f32)
        for d in range(direct):
            x_recv[:, d, 1] = jnp.zeros((ITERS,) + x_recv.shape[3:], f32)

    def prepare():
        for i in LATER:
            copies[i].wait()
        mass_ref[...] = jnp.zeros_like(mass_ref)
        for b in range(blocks):
            at = slice(b * SUB, (b + 1) * SUB)
            lanes = slice(b * block_slots, (b + 1) * block_slots)
            for c in range(parts):
                p_ref[b * SUB + c : b * SUB + c + 1, :block_slots] = p_in[0, c, :, lanes]
            p_ref[at, :] = jnp.where((rows_of(wide) & 3) < 3, doubled(p_ref[at, :]), u_ref[at, :])
            mass_ref[b * SUB + 3 : b * SUB + 4, :] = jnp.ones((1, wide), f32)
            mass_ref[b * SUB + 3 : b * SUB + 4, :block_slots] = mass_in[0, :, lanes]
            mass_ref[at, :] = doubled(mass_ref[at, :])
        op = grad_in[...]
        product = lax.dot_general(
            op, op, (((0,), (0,)), ((), ())), precision=lax.Precision.HIGHEST, preferred_element_type=f32
        )
        high = product.astype(bf16)
        low = (product - high.astype(f32)).astype(bf16)
        gram[...] = jnp.zeros_like(gram)
        for at in (0, node_pad):
            gram[at : at + node_count, :node_count] = high
            gram[at : at + node_count, node_pad : node_pad + node_count] = low
        nodes = jnp.concatenate([nodes_in[0, 0], jnp.full((elements, node_pad - node_count), -1, jnp.int32)], axis=1)
        lists_ref[:elements, :] = nodes.astype(f32)
        stiff_ref[...] = jnp.zeros_like(stiff_ref)
        stiff_ref[:, :elements] = jnp.broadcast_to(stiff_in[0], (stiff_ref.shape[0], elements))
        stiff_ref[...] = jnp.transpose(stiff_ref[...])
        first = rows_of(node_pad) < 4

        def both(source, one):
            here = jnp.broadcast_to(source[one : one + 1, :], (SUB, node_pad))
            return jnp.where(first, here, jnp.broadcast_to(source[one + 1 : one + 2, :], (SUB, node_pad)))

        for one in range(0, elements, 2):
            at = slice(one // 2 * SUB, (one // 2 + 1) * SUB)
            nodes_ref[at, :] = jnp.maximum(both(lists_ref, one), 0.0).astype(jnp.int32)
            scale_ref[at, :] = both(stiff_ref, one)
        columns = jnp.transpose(lists_ref[...]).astype(bf16)
        for one in range(elements):
            b, e = divmod(one, block_elements)
            e_back[b, e * node_pad : (e + 1) * node_pad, :] = spread_columns(columns, one)
        for i in range(others * pairs // LANES):
            c_back[i * LANES : (i + 1) * LANES, :] = spread_columns(columns, contact_row + i)

    def prepare_direct():
        for d in range(direct):
            live = live_in[0, 0, pl.ds(partner(d), 1), :]
            for k in range(pairs // LANES):
                h, at = divmod(k * LANES, pairs // 2)
                code = c_recv[0, d, 4 * h + 3 : 4 * h + 4, at : at + LANES]
                group = jnp.floor(code * (1.0 / wide))
                i = d * (pairs // LANES) + k
                lists_ref[i : i + 1, :] = code - wide * group
                alive = live[:, k * LANES : (k + 1) * LANES] > 0
                which = jnp.where(alive, group.astype(jnp.int32) - 1, -1)
                xb_ref[:, i * LANES : (i + 1) * LANES] = jnp.broadcast_to(which, (SUB, LANES))
        columns = jnp.transpose(lists_ref[...]).astype(bf16)
        for i in range(direct * pairs // LANES):
            x_back[i * LANES : (i + 1) * LANES, :] = spread_columns(columns, i)
        for i in range(2 * ghosts // LANES):
            g_back[i * LANES : (i + 1) * LANES, :] = spread_columns(columns, ghost_row + i)
        total = jnp.zeros((rows, wide), f32)
        width = c_hot.shape[2]
        for at in range(0, direct * pairs, width):
            total = total + put(jnp.ones((SUB, width), f32), c_back, cb_ref, at, width, blocks)
        for b in range(blocks):
            at = slice(b * SUB, (b + 1) * SUB)
            count_ref[at, :] = jnp.where((rows_of(wide) & 3) < 3, PENALTY * doubled(total[at]), 0.0)

    last = segments - 1
    pl.semaphore_wait(
        barrier, others + (direct + 1) * (lax.div(seg + last, segments) + lax.div(last - seg + last, segments))
    )

    row_all = lax.broadcasted_iota(jnp.int32, (rows, wide), 0) & (SUB - 1)
    low_all = row_all < 4

    def split(x):
        high = x.astype(bf16).astype(f32)
        return jnp.where(low_all, high, x - high).astype(bf16)

    def take(packed, hot, which):
        width = which.shape[1]
        picked = dot(packed, hot)
        total = jnp.zeros((SUB, width), f32)
        for b in range(blocks):
            total = jnp.where(which == b, picked[b * SUB : (b + 1) * SUB], total)
        return doubled(total)

    def take_list(packed, d, out_ref):
        width = c_hot.shape[2]
        for at in range(0, pairs // 2, width):
            both = []
            for start in (d * pairs + at, d * pairs + pairs // 2 + at):
                both.append(take(packed, c_hot[start // width], cb_ref[:, start : start + width]))
            out_ref[:, at : at + width] = jnp.where(rows_of(width) < 4, *both)

    def halves(here):
        turned = pltpu.roll(here, 4, 0)
        low = rows_of(here.shape[1]) < 4
        return jnp.where(low, here, turned), jnp.where(low, turned, here)

    def put_list(values, back, base_ref, d, parts, total):
        width = c_hot.shape[2]
        for at in range(0, pairs // 2, width):
            for h, here in enumerate(halves(values[:, at : at + width])):
                total = total + put(here, back, base_ref, d * pairs + h * (pairs // 2) + at, width, parts)
        return total

    def contact_copy(step, d):
        return pltpu.make_async_remote_copy(
            src_ref=c_send.at[d],
            dst_ref=c_recv.at[step, landing(d)],
            send_sem=c_ssem.at[d],
            recv_sem=c_rsem.at[step, landing(d)],
            device_id={"wire": partner(d)},
            device_id_type=MESH,
        )

    def contact_arrival(step, d):
        return pltpu.make_async_remote_copy(
            src_ref=c_send.at[d],
            dst_ref=c_recv.at[step, d],
            send_sem=c_ssem.at[d],
            recv_sem=c_rsem.at[step, d],
            device_id={"wire": partner(d)},
            device_id_type=MESH,
        )

    def ghost_copy(step, side):
        return pltpu.make_async_remote_copy(
            src_ref=g_send.at[side],
            dst_ref=g_recv.at[step, 1 - side],
            send_sem=g_ssem.at[side],
            recv_sem=g_rsem.at[step, 1 - side],
            device_id={"len": seg - 1 if side == 0 else seg + 1},
            device_id_type=MESH,
        )

    def ghost_arrival(step, side):
        return pltpu.make_async_remote_copy(
            src_ref=g_send.at[side],
            dst_ref=g_recv.at[step, side],
            send_sem=g_ssem.at[side],
            recv_sem=g_rsem.at[step, side],
            device_id={"len": seg - 1 if side == 0 else seg + 1},
            device_id_type=MESH,
        )

    def direct_copy(step, d, side):
        return pltpu.make_async_remote_copy(
            src_ref=x_send.at[d, side],
            dst_ref=x_recv.at[step, landing(d), 1 - side],
            send_sem=x_ssem.at[d, side],
            recv_sem=x_rsem.at[step, landing(d), 1 - side],
            device_id={"len": seg - 1 if side == 0 else seg + 1, "wire": partner(d)},
            device_id_type=MESH,
        )

    def direct_arrival(step, d, side):
        return pltpu.make_async_remote_copy(
            src_ref=x_send.at[d, side],
            dst_ref=x_recv.at[step, d, side],
            send_sem=x_ssem.at[d, side],
            recv_sem=x_rsem.at[step, d, side],
            device_id={"len": seg - 1 if side == 0 else seg + 1, "wire": partner(d)},
            device_id_type=MESH,
        )

    exists = (has_prev, has_next)

    def one_step(step, first):
        packed = split(u_ref[...])
        for d in range(others):
            take_list(packed, d, c_send.at[d])
        if first:
            for d in range(others):
                contact_copy(step, d).start()
            prepare()
        else:
            for d in range(direct, others):
                contact_copy(step, d).start()
        for b in range(blocks):
            near, far = u_ref[b * SUB : (b + 1) * SUB, :LANES], u_ref[b * SUB : (b + 1) * SUB, LANES:]
            values = []
            for one in (2 * b, 2 * b + 1):
                slots = nodes_ref[one * SUB : (one + 1) * SUB, :]
                inside = slots & (LANES - 1)
                values.append(jnp.where(slots < LANES, lane_take(near, inside), lane_take(far, inside)))
            values = jnp.concatenate(values, axis=0)
            high = values.astype(bf16)
            at = slice(b * 2 * SUB, (b + 1) * 2 * SUB)
            field[at, :node_pad] = high
            field[at, node_pad:] = (values - high.astype(f32)).astype(bf16)
        reach = blocks * 2 * SUB // 4
        first16 = (lax.broadcasted_iota(jnp.int32, (2 * SUB, node_pad), 0) & (SUB - 1)) < 4
        for at in range(0, blocks * 2 * SUB, reach):
            out = dot(field[at : at + reach, :], gram[...])
            out = (out[:, :node_pad] + out[:, node_pad:]) * scale_ref[at : at + reach, :]
            for i in range(0, reach, 2 * SUB):
                b = (at + i) // (2 * SUB)
                pieces = []
                for j in range(2):
                    r = out[i + j * SUB : i + (j + 1) * SUB]
                    high = r.astype(bf16).astype(f32)
                    r = jnp.concatenate([high, r - high], axis=0)
                    pieces.append(jnp.where(first16, r, 0.0).astype(bf16))
                    pieces.append(jnp.where(first16, 0.0, r).astype(bf16))
                pushed[b * 2 * SUB : (b + 1) * 2 * SUB, :] = jnp.concatenate(pieces, axis=1)
        if not first:
            for d in range(direct):
                total = put_list(c_send[d], x_back, xb_ref, d, 2 * groups, jnp.zeros((2 * groups * SUB, wide), f32))
                total = [doubled(total[i * SUB : (i + 1) * SUB]) for i in range(2 * groups)]
                for side in range(2):
                    mine = total[side * groups : (side + 1) * groups]
                    for i in range(full):
                        x_send[d, side, :, i * wide : (i + 1) * wide] = jnp.where(rows_of(wide) < 4, mine[2 * i], mine[2 * i + 1])
                    if rest:
                        shared = jnp.where(rows_of(LANES) < 4, mine[2 * full][:, :LANES], mine[2 * full][:, LANES:])
                        x_send[d, side, :, full * wide :] = shared
            for side in range(2):

                @pl.when(exists[side])
                def _():
                    for d in range(direct):
                        direct_copy(step, d, side).start()
            for d in reversed(range(direct)):
                contact_copy(step, d).start()

        for b in range(blocks):
            here = dot(pushed[b * 2 * SUB : (b + 1) * 2 * SUB, :], e_back[b])
            part[b * SUB : (b + 1) * SUB, :] = doubled(here[:SUB] + here[SUB:])

        spread = jnp.zeros((rows, wide), f32)
        for d in reversed(range(0 if first else direct, others)):
            contact_arrival(step, d).wait_recv()
            spread = put_list(c_recv[step, d] - c_send[d], c_back, cb_ref, d, blocks, spread)
        inner = (rows_of(wide) & 3) < 3
        for b in range(blocks):
            at = slice(b * SUB, (b + 1) * SUB)
            own = PENALTY * doubled(spread[at]) - part[at, :]
            if not first:
                own = own - count_ref[at, :] * u_ref[at, :]
            part[at, :] = jnp.where(inner, own, mass_ref[at, :])

        picked = take(split(part[...]), g_hot[0], gb_ref[...])
        for side in range(2):
            at = side * ghosts
            g_send[side] = jnp.where(rows_of(half) < 4, picked[:, at : at + half], picked[:, at + half : at + ghosts])
        for side in range(2):

            @pl.when(exists[side])
            def _():
                ghost_copy(step, side).start()

        if first:
            prepare_direct()
        else:
            spread = jnp.zeros((rows, wide), f32)
            for d in range(direct):
                contact_arrival(step, d).wait_recv()
                spread = put_list(c_recv[step, d], c_back, cb_ref, d, blocks, spread)
            for b in range(blocks):
                at = slice(b * SUB, (b + 1) * SUB)
                part[at, :] = part[at, :] + jnp.where(inner, PENALTY * doubled(spread[at]), 0.0)

        for side in range(2):

            @pl.when(exists[side])
            def _():
                ghost_arrival(step, side).wait_recv()
                for d in range(0 if first else direct):
                    direct_arrival(step, d, side).wait_recv()

        arrived = []
        for side in range(2):
            here = g_recv[step, side]
            if not first:
                crossed = sum(x_recv[step, d, side] for d in range(direct))
                here = here + jnp.where((rows_of(half) & 3) < 3, PENALTY * crossed, 0.0)
            arrived += halves(here)
        spread = put(jnp.concatenate(arrived, axis=1), g_back, gb_ref, 0, 2 * ghosts, blocks)
        for b in range(blocks):
            at = slice(b * SUB, (b + 1) * SUB)
            part[at, :] = part[at, :] + doubled(spread[at])

        if first:
            for b in range(blocks):
                mass = jnp.broadcast_to(part[b * SUB + 3 : b * SUB + 4, :], (SUB, wide))
                rate_ref[b * SUB : (b + 1) * SUB, :] = jnp.where(inner, TIME_SQUARE / mass, 0.0)

        now = u_ref[...]
        u_ref[...] = 2.0 * now - p_ref[...] + rate_ref[...] * part[...]
        p_ref[...] = now

        for d in range(others):
            contact_copy(step, d).wait_send()
        for side in range(2):

            @pl.when(exists[side])
            def _():
                ghost_copy(step, side).wait_send()
                for d in range(0 if first else direct):
                    direct_copy(step, d, side).wait_send()

    one_step(0, True)

    def later_step(step, _):
        one_step(step, False)
        return 0

    lax.fori_loop(1, ITERS, later_step, 0)
    for b in range(blocks):
        lanes = slice(b * block_slots, (b + 1) * block_slots)
        for c in range(parts):
            row = slice(b * SUB + c, b * SUB + c + 1)
            u_out[0, c, :, lanes] = u_ref[row, :block_slots]
            p_out[0, c, :, lanes] = p_ref[row, :block_slots]


def hand_on(u_from, p_from, u_to, p_to):
    u_to[...] = u_from[...]
    p_to[...] = p_from[...]


def on_device(displacement, previous, element_nodes, *rest):
    left_ghost, contact_slots = rest[3], rest[5]
    node_count, elements = element_nodes.shape[2:]
    blocks = elements // block_elements
    wide = round_up(block_slots, 2 * LANES)
    node_pad = round_up(node_count, LANES)
    wires = lax.axis_size("wire")
    others = wires - 1
    rows = blocks * SUB
    pairs = contact_slots.shape[3]
    ghosts = left_ghost.shape[2]
    c_width = 512 if pairs % 1024 == 0 else pairs // 2
    mirrored = wires & (wires - 1) == 0
    direct = others - 1 if mirrored else others
    groups = 2 * (ghosts // 2 // wide) + (ghosts // 2 % wide > 0)
    assert block_elements == 4 and node_pad == LANES and wide == 2 * LANES and blocks % 4 == 0
    assert elements + others * pairs // LANES + 2 * ghosts // LANES <= LANES
    assert direct > 0 and ghosts // 2 % wide in (0, LANES) and direct * pairs <= LANES * LANES
    assert wide * (2 * groups + 1) < 65536
    assert all((x * BLOCK_SCALE) >> BLOCK_SHIFT == x // block_slots for x in range(blocks * block_slots))

    vmem = pl.BlockSpec(memory_space=pltpu.VMEM)
    turned = jnp.swapaxes(displacement, 1, 2)
    args = (turned, jnp.swapaxes(previous, 1, 2), jnp.swapaxes(element_nodes, 2, 3), *rest)
    results = pl.pallas_call(
        functools.partial(step_kernel, wires, lax.axis_size("len"), 512),
        out_shape=[jax.ShapeDtypeStruct(turned.shape, f32)] * 2,
        in_specs=[pl.BlockSpec(memory_space=pl.ANY)] * len(args),
        out_specs=[vmem] * 2,
        scratch_shapes=[pltpu.VMEM(x.shape, x.dtype) for x in args]
        + [pltpu.SemaphoreType.DMA((len(args),))]
        + [
            pltpu.VMEM((rows, wide), f32),
            pltpu.VMEM((rows, wide), f32),
            pltpu.VMEM((rows, wide), f32),
            pltpu.VMEM((rows, wide), f32),
            pltpu.VMEM((others * pairs // c_width, wide, c_width), bf16),
            pltpu.VMEM((1, wide, 2 * ghosts), bf16),
            pltpu.VMEM((others * pairs, wide), bf16),
            pltpu.VMEM((2 * ghosts, wide), bf16),
            pltpu.VMEM((direct * pairs, wide), bf16),
            pltpu.VMEM((blocks, block_elements * node_pad, wide), bf16),
            pltpu.VMEM((SUB, others * pairs), jnp.int32),
            pltpu.VMEM((SUB, 2 * ghosts), jnp.int32),
            pltpu.VMEM((SUB, direct * pairs), jnp.int32),
            pltpu.VMEM((rows, wide), f32),
            pltpu.VMEM((2 * node_pad, 2 * node_pad), bf16),
            pltpu.VMEM((elements // 2 * SUB, node_pad), jnp.int32),
            pltpu.VMEM((LANES, LANES), f32),
            pltpu.VMEM((LANES, LANES), f32),
            pltpu.VMEM((elements // 2 * SUB, node_pad), f32),
            pltpu.VMEM((rows, wide), f32),
            pltpu.VMEM((elements // 2 * SUB, 2 * node_pad), bf16),
            pltpu.VMEM((blocks * 2 * SUB, block_elements * node_pad), bf16),
            pltpu.VMEM((others, SUB, pairs // 2), f32),
            pltpu.VMEM((ITERS, others, SUB, pairs // 2), f32),
            pltpu.VMEM((2, SUB, ghosts // 2), f32),
            pltpu.VMEM((ITERS, 2, SUB, ghosts // 2), f32),
            pltpu.VMEM((direct, 2, SUB, ghosts // 2), f32),
            pltpu.VMEM((ITERS, direct, 2, SUB, ghosts // 2), f32),
            pltpu.SemaphoreType.DMA((others,)),
            pltpu.SemaphoreType.DMA((ITERS, others)),
            pltpu.SemaphoreType.DMA((2,)),
            pltpu.SemaphoreType.DMA((ITERS, 2)),
            pltpu.SemaphoreType.DMA((direct, 2)),
            pltpu.SemaphoreType.DMA((ITERS, direct, 2)),
        ],
        compiler_params=pltpu.CompilerParams(
            collective_id=0, has_side_effects=True, vmem_limit_bytes=VMEM_BYTES
        ),
        name="steps",
    )(*args)
    results = pl.pallas_call(
        hand_on,
        out_shape=[jax.ShapeDtypeStruct(turned.shape, f32)] * 2,
        in_specs=[vmem] * 2,
        out_specs=[vmem] * 2,
        name="hand_on",
    )(*results)
    return tuple(jnp.swapaxes(x, 1, 2) for x in results)


def solution(mesh):
    four = P("len", "wire", None, None)
    three = P("len", "wire", None)
    return jax.shard_map(
        on_device,
        mesh=mesh,
        in_specs=(four, four, four, three, P(), three, three, three, four, four),
        out_specs=(four, four),
        check_vma=False,
    )
```

```python
import functools

import jax
import jax.numpy as jnp
from jax import lax
from jax.experimental import pallas as pl
from jax.experimental.pallas import tpu as pltpu
from jax.sharding import PartitionSpec as P

ITERS = 4
PENALTY = 4.0
TIME_SQUARE = 0.03
block_slots = 224
block_elements = 4
LANES = 128
ARGS = 10
VMEM_BYTES = 67_043_328
FIRST = (6, 7, 8, 9, 0)
LATER = (1, 2, 3, 4, 5)
BLOCK_SCALE, BLOCK_SHIFT = 4682, 20
SUB = 8
f32 = jnp.float32
bf16 = jnp.bfloat16
MESH = pl.DeviceIdType.MESH


def round_up(value, step):
    return -(-value // step) * step


def dot(a, b):
    return jnp.dot(a, b, preferred_element_type=f32)


def dot_nt(a, b):
    return lax.dot_general(a, b, (((1,), (1,)), ((), ())), preferred_element_type=f32)


def lane_take(values, lanes):
    return jnp.take_along_axis(values, lanes, axis=1, mode="promise_in_bounds")


def step_kernel(
    wires,
    segments,
    chunk,
    *refs,
):
    sources, refs = refs[:ARGS], refs[ARGS:]
    inputs, in_sem, refs = refs[2 : 2 + ARGS], refs[2 + ARGS], refs[:2] + refs[3 + ARGS :]
    copies = [
        pltpu.make_async_copy(source, target, in_sem.at[i])
        for i, (source, target) in enumerate(zip(sources, inputs))
    ]
    for i in FIRST + LATER:
        copies[i].start()
    run(wires, segments, chunk, copies, *inputs, *refs)


def run(
    wires,
    segments,
    chunk,
    copies,
    u_in, p_in, nodes_in, stiff_in, grad_in, mass_in, left_in, right_in, slots_in, live_in,
    u_out, p_out,
    u_ref, p_ref, mass_ref, rate_ref,
    c_hot, g_hot, c_back, g_back, x_back, e_back, cb_ref, gb_ref, xb_ref, count_ref, gram, nodes_ref, lists_ref, stiff_ref, scale_ref,
    part, field, pushed, c_send, c_recv, g_send, g_recv, x_send, x_recv,
    c_ssem, c_rsem, g_ssem, g_rsem, x_ssem, x_rsem,
):
    others = wires - 1
    direct = x_send.shape[0]
    blocks = e_back.shape[0]
    parts = u_in.shape[1]
    rows, wide = u_ref.shape
    pairs = slots_in.shape[3]
    ghosts = left_in.shape[2]
    elements, node_count = nodes_in.shape[2:]
    node_pad = gram.shape[0] // 2
    contact_row = elements
    ghost_row = contact_row + others * pairs // LANES
    me = lax.axis_index("wire")
    seg = lax.axis_index("len")
    has_prev = seg > 0
    has_next = seg < segments - 1
    half = ghosts // 2
    full, rest = divmod(half, wide)
    places = [(h * half + i * wide, wide, 2 * i + h, 0) for i in range(full) for h in range(2)]
    places += [(h * half + full * wide, rest, 2 * full, h * LANES) for h in range(2) if rest]
    groups = 2 * full + (rest > 0)
    mirrored = wires & (wires - 1) == 0

    def partner(d):
        if not mirrored:
            return lax.rem(me + (d + 1), wires)
        offset, other, bit = wires - 1 - d, me, 1
        while bit <= offset:
            if offset & bit:
                other = other + bit - 2 * bit * lax.rem(lax.div(me, bit), 2)
            bit *= 2
        return other

    def landing(d):
        return d if mirrored else others - 1 - d

    barrier = pltpu.get_barrier_semaphore()
    for d in range(others):
        pl.semaphore_signal(barrier, inc=1, device_id={"wire": partner(d)}, device_id_type=MESH)

    @pl.when(has_prev)
    def _():
        pl.semaphore_signal(barrier, inc=1, device_id={"len": seg - 1}, device_id_type=MESH)
        for d in range(direct):
            there = {"len": seg - 1, "wire": partner(d)}
            pl.semaphore_signal(barrier, inc=1, device_id=there, device_id_type=MESH)

    @pl.when(has_next)
    def _():
        pl.semaphore_signal(barrier, inc=1, device_id={"len": seg + 1}, device_id_type=MESH)
        for d in range(direct):
            there = {"len": seg + 1, "wire": partner(d)}
            pl.semaphore_signal(barrier, inc=1, device_id=there, device_id_type=MESH)

    def rows_of(width):
        return lax.broadcasted_iota(jnp.int32, (SUB, width), 0)

    def doubled(x):
        return x + pltpu.roll(x, 4, 0)

    def placed(values, base_ref, start, width, parts):
        high = values.astype(bf16).astype(f32)
        values = jnp.where(rows_of(width) < 4, high, values - high)
        which = base_ref[:, start : start + width]
        return jnp.concatenate([jnp.where(which == b, values, 0.0) for b in range(parts)], axis=0).astype(bf16)

    def put(values, back, base_ref, start, width, parts):
        return dot(placed(values, base_ref, start, width, parts), back[start : start + width, :])

    def match(slots):
        ids = lax.broadcasted_iota(jnp.int32, (wide, LANES), 0).astype(bf16)
        here = jnp.broadcast_to(slots.astype(f32), (2 * SUB, LANES)).astype(bf16)
        here = jnp.concatenate([here] * (wide // (2 * SUB)), axis=0)
        return jnp.where(ids == here, jnp.ones((), bf16), jnp.zeros((), bf16))

    def block_of(slots):
        return (slots * BLOCK_SCALE) >> BLOCK_SHIFT

    def spread_columns(columns, at):
        lanes = lax.broadcasted_iota(jnp.int32, (LANES, wide), 1).astype(bf16)
        here = jnp.broadcast_to(columns[:, at : at + 1], (LANES, wide))
        return jnp.where(lanes == here, jnp.ones((), bf16), jnp.zeros((), bf16))

    def fill(hot, base_ref, at, slots, live, row):
        count = slots.shape[1]
        which = block_of(slots)
        inside = slots - which * block_slots
        if live is not None:
            which = jnp.where(live > 0, which, -1)
        base_ref[:, at : at + count] = jnp.broadcast_to(which, (SUB, count))
        for start in range(0, count, LANES):
            here = inside[:, start : start + LANES]
            group, lane = divmod(at + start, hot.shape[2])
            hot[group, :, lane : lane + LANES] = match(here)
            at_row = row + (at + start) // LANES
            lists_ref[at_row : at_row + 1, :] = here.astype(f32)

    for i in FIRST:
        copies[i].wait()
    u_ref[...] = jnp.zeros_like(u_ref)
    p_ref[...] = jnp.zeros_like(p_ref)
    lists_ref[...] = jnp.zeros_like(lists_ref)
    for b in range(blocks):
        lanes = slice(b * block_slots, (b + 1) * block_slots)
        for c in range(parts):
            row = slice(b * SUB + c, b * SUB + c + 1)
            u_ref[row, :block_slots] = u_in[0, c, :, lanes]
    fill(g_hot, gb_ref, 0, left_in[0], None, ghost_row)
    fill(g_hot, gb_ref, ghosts, right_in[0], None, ghost_row)
    codes = []
    for side in range(2):
        for _, count, group, at in sorted(places):
            code = lax.broadcasted_iota(jnp.int32, (SUB, count), 1) + (wide * (side * groups + group + 1) + at)
            codes.append(code.astype(f32))
    codes = jnp.concatenate(codes, axis=1)
    last_row = (rows_of(wide) & 3) == 3
    codes = dot_nt(placed(codes, gb_ref, 0, 2 * ghosts, blocks), g_hot[0])
    for b in range(blocks):
        at = slice(b * SUB, (b + 1) * SUB)
        u_ref[at, :] = jnp.where(last_row, doubled(codes[at]), doubled(u_ref[at, :]))
    for d in range(others):
        fill(c_hot, cb_ref, d * pairs, slots_in[0, 0, pl.ds(partner(d), 1), :], live_in[0, 0, pl.ds(partner(d), 1), :], contact_row)

    @pl.when(jnp.logical_not(has_prev))
    def _():
        g_recv[:, 0] = jnp.zeros((ITERS,) + g_recv.shape[2:], f32)
        for d in range(direct):
            x_recv[:, d, 0] = jnp.zeros((ITERS,) + x_recv.shape[3:], f32)

    @pl.when(jnp.logical_not(has_next))
    def _():
        g_recv[:, 1] = jnp.zeros((ITERS,) + g_recv.shape[2:], f32)
        for d in range(direct):
            x_recv[:, d, 1] = jnp.zeros((ITERS,) + x_recv.shape[3:], f32)

    def prepare():
        for i in LATER:
            copies[i].wait()
        mass_ref[...] = jnp.zeros_like(mass_ref)
        for b in range(blocks):
            at = slice(b * SUB, (b + 1) * SUB)
            lanes = slice(b * block_slots, (b + 1) * block_slots)
            for c in range(parts):
                p_ref[b * SUB + c : b * SUB + c + 1, :block_slots] = p_in[0, c, :, lanes]
            p_ref[at, :] = jnp.where((rows_of(wide) & 3) < 3, doubled(p_ref[at, :]), u_ref[at, :])
            mass_ref[b * SUB + 3 : b * SUB + 4, :] = jnp.ones((1, wide), f32)
            mass_ref[b * SUB + 3 : b * SUB + 4, :block_slots] = mass_in[0, :, lanes]
            mass_ref[at, :] = doubled(mass_ref[at, :])
        op = grad_in[...]
        product = lax.dot_general(
            op, op, (((0,), (0,)), ((), ())), precision=lax.Precision.HIGHEST, preferred_element_type=f32
        )
        high = product.astype(bf16)
        low = (product - high.astype(f32)).astype(bf16)
        gram[...] = jnp.zeros_like(gram)
        for at in (0, node_pad):
            gram[at : at + node_count, :node_count] = high
            gram[at : at + node_count, node_pad : node_pad + node_count] = low
        nodes = jnp.concatenate([nodes_in[0, 0], jnp.full((elements, node_pad - node_count), -1, jnp.int32)], axis=1)
        lists_ref[:elements, :] = nodes.astype(f32)
        stiff_ref[...] = jnp.zeros_like(stiff_ref)
        stiff_ref[:, :elements] = jnp.broadcast_to(stiff_in[0], (stiff_ref.shape[0], elements))
        stiff_ref[...] = jnp.transpose(stiff_ref[...])
        first = rows_of(node_pad) < 4

        def both(source, one):
            here = jnp.broadcast_to(source[one : one + 1, :], (SUB, node_pad))
            return jnp.where(first, here, jnp.broadcast_to(source[one + 1 : one + 2, :], (SUB, node_pad)))

        for one in range(0, elements, 2):
            at = slice(one // 2 * SUB, (one // 2 + 1) * SUB)
            nodes_ref[at, :] = jnp.maximum(both(lists_ref, one), 0.0).astype(jnp.int32)
            scale_ref[at, :] = both(stiff_ref, one)
        columns = jnp.transpose(lists_ref[...]).astype(bf16)
        for one in range(elements):
            b, e = divmod(one, block_elements)
            e_back[b, e * node_pad : (e + 1) * node_pad, :] = spread_columns(columns, one)
        for i in range(others * pairs // LANES):
            c_back[i * LANES : (i + 1) * LANES, :] = spread_columns(columns, contact_row + i)

    def prepare_direct():
        for d in range(direct):
            live = live_in[0, 0, pl.ds(partner(d), 1), :]
            for k in range(pairs // LANES):
                h, at = divmod(k * LANES, pairs // 2)
                code = c_recv[0, d, 4 * h + 3 : 4 * h + 4, at : at + LANES]
                group = jnp.floor(code * (1.0 / wide))
                i = d * (pairs // LANES) + k
                lists_ref[i : i + 1, :] = code - wide * group
                alive = live[:, k * LANES : (k + 1) * LANES] > 0
                which = jnp.where(alive, group.astype(jnp.int32) - 1, -1)
                xb_ref[:, i * LANES : (i + 1) * LANES] = jnp.broadcast_to(which, (SUB, LANES))
        columns = jnp.transpose(lists_ref[...]).astype(bf16)
        for i in range(direct * pairs // LANES):
            x_back[i * LANES : (i + 1) * LANES, :] = spread_columns(columns, i)
        for i in range(2 * ghosts // LANES):
            g_back[i * LANES : (i + 1) * LANES, :] = spread_columns(columns, ghost_row + i)
        total = jnp.zeros((rows, wide), f32)
        width = c_hot.shape[2]
        for at in range(0, direct * pairs, width):
            total = total + put(jnp.ones((SUB, width), f32), c_back, cb_ref, at, width, blocks)
        for b in range(blocks):
            at = slice(b * SUB, (b + 1) * SUB)
            count_ref[at, :] = jnp.where((rows_of(wide) & 3) < 3, PENALTY * doubled(total[at]), 0.0)

    def entry():
        last = segments - 1
        pl.semaphore_wait(
            barrier, others + (direct + 1) * (lax.div(seg + last, segments) + lax.div(last - seg + last, segments))
        )

    row_all = lax.broadcasted_iota(jnp.int32, (rows, wide), 0) & (SUB - 1)
    low_all = row_all < 4

    def split(x):
        high = x.astype(bf16).astype(f32)
        return jnp.where(low_all, high, x - high).astype(bf16)

    def take(packed, hot, which):
        width = which.shape[1]
        picked = dot(packed, hot)
        total = jnp.zeros((SUB, width), f32)
        for b in range(blocks):
            total = jnp.where(which == b, picked[b * SUB : (b + 1) * SUB], total)
        return doubled(total)

    def take_list(packed, d, out_ref):
        width = c_hot.shape[2]
        for at in range(0, pairs // 2, width):
            both = []
            for start in (d * pairs + at, d * pairs + pairs // 2 + at):
                both.append(take(packed, c_hot[start // width], cb_ref[:, start : start + width]))
            out_ref[:, at : at + width] = jnp.where(rows_of(width) < 4, *both)

    def halves(here):
        turned = pltpu.roll(here, 4, 0)
        low = rows_of(here.shape[1]) < 4
        return jnp.where(low, here, turned), jnp.where(low, turned, here)

    def put_list(values, back, base_ref, d, parts, total):
        width = c_hot.shape[2]
        for at in range(0, pairs // 2, width):
            for h, here in enumerate(halves(values[:, at : at + width])):
                total = total + put(here, back, base_ref, d * pairs + h * (pairs // 2) + at, width, parts)
        return total

    def contact_copy(step, d):
        return pltpu.make_async_remote_copy(
            src_ref=c_send.at[d],
            dst_ref=c_recv.at[step, landing(d)],
            send_sem=c_ssem.at[d],
            recv_sem=c_rsem.at[step, landing(d)],
            device_id={"wire": partner(d)},
            device_id_type=MESH,
        )

    def contact_arrival(step, d):
        return pltpu.make_async_remote_copy(
            src_ref=c_send.at[d],
            dst_ref=c_recv.at[step, d],
            send_sem=c_ssem.at[d],
            recv_sem=c_rsem.at[step, d],
            device_id={"wire": partner(d)},
            device_id_type=MESH,
        )

    def ghost_copy(step, side):
        return pltpu.make_async_remote_copy(
            src_ref=g_send.at[side],
            dst_ref=g_recv.at[step, 1 - side],
            send_sem=g_ssem.at[side],
            recv_sem=g_rsem.at[step, 1 - side],
            device_id={"len": seg - 1 if side == 0 else seg + 1},
            device_id_type=MESH,
        )

    def ghost_arrival(step, side):
        return pltpu.make_async_remote_copy(
            src_ref=g_send.at[side],
            dst_ref=g_recv.at[step, side],
            send_sem=g_ssem.at[side],
            recv_sem=g_rsem.at[step, side],
            device_id={"len": seg - 1 if side == 0 else seg + 1},
            device_id_type=MESH,
        )

    def direct_copy(step, d, side):
        return pltpu.make_async_remote_copy(
            src_ref=x_send.at[d, side],
            dst_ref=x_recv.at[step, landing(d), 1 - side],
            send_sem=x_ssem.at[d, side],
            recv_sem=x_rsem.at[step, landing(d), 1 - side],
            device_id={"len": seg - 1 if side == 0 else seg + 1, "wire": partner(d)},
            device_id_type=MESH,
        )

    def direct_arrival(step, d, side):
        return pltpu.make_async_remote_copy(
            src_ref=x_send.at[d, side],
            dst_ref=x_recv.at[step, d, side],
            send_sem=x_ssem.at[d, side],
            recv_sem=x_rsem.at[step, d, side],
            device_id={"len": seg - 1 if side == 0 else seg + 1, "wire": partner(d)},
            device_id_type=MESH,
        )

    exists = (has_prev, has_next)
    far_first = list(range(1, direct)) + [0] + list(range(direct, others))

    def one_step(step, first):
        packed = split(u_ref[...])
        for d in range(others):
            take_list(packed, d, c_send.at[d])
        if first:
            entry()
            for d in far_first:
                contact_copy(step, d).start()
            prepare()
        else:
            for d in far_first:
                contact_copy(step, d).start()
        for b in range(blocks):
            near, far = u_ref[b * SUB : (b + 1) * SUB, :LANES], u_ref[b * SUB : (b + 1) * SUB, LANES:]
            values = []
            for one in (2 * b, 2 * b + 1):
                slots = nodes_ref[one * SUB : (one + 1) * SUB, :]
                inside = slots & (LANES - 1)
                values.append(jnp.where(slots < LANES, lane_take(near, inside), lane_take(far, inside)))
            values = jnp.concatenate(values, axis=0)
            high = values.astype(bf16)
            at = slice(b * 2 * SUB, (b + 1) * 2 * SUB)
            field[at, :node_pad] = high
            field[at, node_pad:] = (values - high.astype(f32)).astype(bf16)
        reach = blocks * 2 * SUB // 4
        first16 = (lax.broadcasted_iota(jnp.int32, (2 * SUB, node_pad), 0) & (SUB - 1)) < 4
        for at in range(0, blocks * 2 * SUB, reach):
            out = dot(field[at : at + reach, :], gram[...])
            out = (out[:, :node_pad] + out[:, node_pad:]) * scale_ref[at : at + reach, :]
            for i in range(0, reach, 2 * SUB):
                b = (at + i) // (2 * SUB)
                pieces = []
                for j in range(2):
                    r = out[i + j * SUB : i + (j + 1) * SUB]
                    high = r.astype(bf16).astype(f32)
                    r = jnp.concatenate([high, r - high], axis=0)
                    pieces.append(jnp.where(first16, r, 0.0).astype(bf16))
                    pieces.append(jnp.where(first16, 0.0, r).astype(bf16))
                pushed[b * 2 * SUB : (b + 1) * 2 * SUB, :] = jnp.concatenate(pieces, axis=1)
        if not first:
            for d in range(direct):
                total = put_list(c_send[d], x_back, xb_ref, d, 2 * groups, jnp.zeros((2 * groups * SUB, wide), f32))
                total = [doubled(total[i * SUB : (i + 1) * SUB]) for i in range(2 * groups)]
                for side in range(2):
                    mine = total[side * groups : (side + 1) * groups]
                    for i in range(full):
                        x_send[d, side, :, i * wide : (i + 1) * wide] = jnp.where(rows_of(wide) < 4, mine[2 * i], mine[2 * i + 1])
                    if rest:
                        shared = jnp.where(rows_of(LANES) < 4, mine[2 * full][:, :LANES], mine[2 * full][:, LANES:])
                        x_send[d, side, :, full * wide :] = shared
            for side in range(2):

                @pl.when(exists[side])
                def _():
                    for d in range(direct):
                        direct_copy(step, d, side).start()

        for b in range(blocks):
            here = dot(pushed[b * 2 * SUB : (b + 1) * 2 * SUB, :], e_back[b])
            part[b * SUB : (b + 1) * SUB, :] = doubled(here[:SUB] + here[SUB:])

        spread = jnp.zeros((rows, wide), f32)
        for d in reversed(far_first if first else range(direct, others)):
            contact_arrival(step, d).wait_recv()
            spread = put_list(c_recv[step, d] - c_send[d], c_back, cb_ref, d, blocks, spread)
        inner = (rows_of(wide) & 3) < 3
        for b in range(blocks):
            at = slice(b * SUB, (b + 1) * SUB)
            own = PENALTY * doubled(spread[at]) - part[at, :]
            if not first:
                own = own - count_ref[at, :] * u_ref[at, :]
            part[at, :] = jnp.where(inner, own, mass_ref[at, :])

        picked = take(split(part[...]), g_hot[0], gb_ref[...])
        for side in range(2):
            at = side * ghosts
            g_send[side] = jnp.where(rows_of(half) < 4, picked[:, at : at + half], picked[:, at + half : at + ghosts])
        for side in range(2):

            @pl.when(exists[side])
            def _():
                ghost_copy(step, side).start()

        if first:
            prepare_direct()
        else:
            spread = jnp.zeros((rows, wide), f32)
            for d in range(direct):
                contact_arrival(step, d).wait_recv()
                spread = put_list(c_recv[step, d], c_back, cb_ref, d, blocks, spread)
            for b in range(blocks):
                at = slice(b * SUB, (b + 1) * SUB)
                part[at, :] = part[at, :] + jnp.where(inner, PENALTY * doubled(spread[at]), 0.0)

        for side in range(2):

            @pl.when(exists[side])
            def _():
                ghost_arrival(step, side).wait_recv()
                for d in range(0 if first else direct):
                    direct_arrival(step, d, side).wait_recv()

        arrived = []
        for side in range(2):
            here = g_recv[step, side]
            if not first:
                crossed = sum(x_recv[step, d, side] for d in range(direct))
                here = here + jnp.where((rows_of(half) & 3) < 3, PENALTY * crossed, 0.0)
            arrived += halves(here)
        spread = put(jnp.concatenate(arrived, axis=1), g_back, gb_ref, 0, 2 * ghosts, blocks)
        for b in range(blocks):
            at = slice(b * SUB, (b + 1) * SUB)
            part[at, :] = part[at, :] + doubled(spread[at])

        if first:
            for b in range(blocks):
                mass = jnp.broadcast_to(part[b * SUB + 3 : b * SUB + 4, :], (SUB, wide))
                rate_ref[b * SUB : (b + 1) * SUB, :] = jnp.where(inner, TIME_SQUARE / mass, 0.0)

        now = u_ref[...]
        u_ref[...] = 2.0 * now - p_ref[...] + rate_ref[...] * part[...]
        p_ref[...] = now

        for d in range(others):
            contact_copy(step, d).wait_send()
        for side in range(2):

            @pl.when(exists[side])
            def _():
                ghost_copy(step, side).wait_send()
                for d in range(0 if first else direct):
                    direct_copy(step, d, side).wait_send()

    one_step(0, True)

    def later_step(step, _):
        one_step(step, False)
        return 0

    lax.fori_loop(1, ITERS, later_step, 0)
    for b in range(blocks):
        lanes = slice(b * block_slots, (b + 1) * block_slots)
        for c in range(parts):
            row = slice(b * SUB + c, b * SUB + c + 1)
            u_out[0, c, :, lanes] = u_ref[row, :block_slots]
            p_out[0, c, :, lanes] = p_ref[row, :block_slots]


def hand_on(u_from, p_from, u_to, p_to):
    u_to[...] = u_from[...]
    p_to[...] = p_from[...]


def on_device(displacement, previous, element_nodes, *rest):
    left_ghost, contact_slots = rest[3], rest[5]
    node_count, elements = element_nodes.shape[2:]
    blocks = elements // block_elements
    wide = round_up(block_slots, 2 * LANES)
    node_pad = round_up(node_count, LANES)
    wires = lax.axis_size("wire")
    others = wires - 1
    rows = blocks * SUB
    pairs = contact_slots.shape[3]
    ghosts = left_ghost.shape[2]
    c_width = 512 if pairs % 1024 == 0 else pairs // 2
    mirrored = wires & (wires - 1) == 0
    direct = others - 1 if mirrored else others
    groups = 2 * (ghosts // 2 // wide) + (ghosts // 2 % wide > 0)
    assert block_elements == 4 and node_pad == LANES and wide == 2 * LANES and blocks % 4 == 0
    assert elements + others * pairs // LANES + 2 * ghosts // LANES <= LANES
    assert direct > 0 and ghosts // 2 % wide in (0, LANES) and direct * pairs <= LANES * LANES
    assert wide * (2 * groups + 1) < 65536
    assert all((x * BLOCK_SCALE) >> BLOCK_SHIFT == x // block_slots for x in range(blocks * block_slots))

    vmem = pl.BlockSpec(memory_space=pltpu.VMEM)
    turned = jnp.swapaxes(displacement, 1, 2)
    args = (turned, jnp.swapaxes(previous, 1, 2), jnp.swapaxes(element_nodes, 2, 3), *rest)
    results = pl.pallas_call(
        functools.partial(step_kernel, wires, lax.axis_size("len"), 512),
        out_shape=[jax.ShapeDtypeStruct(turned.shape, f32)] * 2,
        in_specs=[pl.BlockSpec(memory_space=pl.ANY)] * len(args),
        out_specs=[vmem] * 2,
        scratch_shapes=[pltpu.VMEM(x.shape, x.dtype) for x in args]
        + [pltpu.SemaphoreType.DMA((len(args),))]
        + [
            pltpu.VMEM((rows, wide), f32),
            pltpu.VMEM((rows, wide), f32),
            pltpu.VMEM((rows, wide), f32),
            pltpu.VMEM((rows, wide), f32),
            pltpu.VMEM((others * pairs // c_width, wide, c_width), bf16),
            pltpu.VMEM((1, wide, 2 * ghosts), bf16),
            pltpu.VMEM((others * pairs, wide), bf16),
            pltpu.VMEM((2 * ghosts, wide), bf16),
            pltpu.VMEM((direct * pairs, wide), bf16),
            pltpu.VMEM((blocks, block_elements * node_pad, wide), bf16),
            pltpu.VMEM((SUB, others * pairs), jnp.int32),
            pltpu.VMEM((SUB, 2 * ghosts), jnp.int32),
            pltpu.VMEM((SUB, direct * pairs), jnp.int32),
            pltpu.VMEM((rows, wide), f32),
            pltpu.VMEM((2 * node_pad, 2 * node_pad), bf16),
            pltpu.VMEM((elements // 2 * SUB, node_pad), jnp.int32),
            pltpu.VMEM((LANES, LANES), f32),
            pltpu.VMEM((LANES, LANES), f32),
            pltpu.VMEM((elements // 2 * SUB, node_pad), f32),
            pltpu.VMEM((rows, wide), f32),
            pltpu.VMEM((elements // 2 * SUB, 2 * node_pad), bf16),
            pltpu.VMEM((blocks * 2 * SUB, block_elements * node_pad), bf16),
            pltpu.VMEM((others, SUB, pairs // 2), f32),
            pltpu.VMEM((ITERS, others, SUB, pairs // 2), f32),
            pltpu.VMEM((2, SUB, ghosts // 2), f32),
            pltpu.VMEM((ITERS, 2, SUB, ghosts // 2), f32),
            pltpu.VMEM((direct, 2, SUB, ghosts // 2), f32),
            pltpu.VMEM((ITERS, direct, 2, SUB, ghosts // 2), f32),
            pltpu.SemaphoreType.DMA((others,)),
            pltpu.SemaphoreType.DMA((ITERS, others)),
            pltpu.SemaphoreType.DMA((2,)),
            pltpu.SemaphoreType.DMA((ITERS, 2)),
            pltpu.SemaphoreType.DMA((direct, 2)),
            pltpu.SemaphoreType.DMA((ITERS, direct, 2)),
        ],
        compiler_params=pltpu.CompilerParams(
            collective_id=0, has_side_effects=True, vmem_limit_bytes=VMEM_BYTES
        ),
        name="steps",
    )(*args)
    results = pl.pallas_call(
        hand_on,
        out_shape=[jax.ShapeDtypeStruct(turned.shape, f32)] * 2,
        in_specs=[vmem] * 2,
        out_specs=[vmem] * 2,
        name="hand_on",
    )(*results)
    return tuple(jnp.swapaxes(x, 1, 2) for x in results)


def solution(mesh):
    four = P("len", "wire", None, None)
    three = P("len", "wire", None)
    return jax.shard_map(
        on_device,
        mesh=mesh,
        in_specs=(four, four, four, three, P(), three, three, three, four, four),
        out_specs=(four, four),
        check_vma=False,
    )
```

```python
import functools

import jax
import jax.numpy as jnp
from jax import lax
from jax.experimental import pallas as pl
from jax.experimental.pallas import tpu as pltpu
from jax.sharding import PartitionSpec as P

ITERS = 4
PENALTY = 4.0
TIME_SQUARE = 0.03
block_slots = 224
block_elements = 4
LANES = 128
ARGS = 10
VMEM_BYTES = 67_043_328
FIRST = (6, 7, 8, 9, 0)
LATER = (1, 2, 3, 4, 5)
BLOCK_SCALE, BLOCK_SHIFT = 4682, 20
SUB = 8
f32 = jnp.float32
bf16 = jnp.bfloat16
MESH = pl.DeviceIdType.MESH


def round_up(value, step):
    return -(-value // step) * step


def dot(a, b):
    return jnp.dot(a, b, preferred_element_type=f32)


def dot_nt(a, b):
    return lax.dot_general(a, b, (((1,), (1,)), ((), ())), preferred_element_type=f32)


def lane_take(values, lanes):
    return jnp.take_along_axis(values, lanes, axis=1, mode="promise_in_bounds")


def step_kernel(
    wires,
    segments,
    chunk,
    *refs,
):
    sources, refs = refs[:ARGS], refs[ARGS:]
    inputs, in_sem, refs = refs[2 : 2 + ARGS], refs[2 + ARGS], refs[:2] + refs[3 + ARGS :]
    copies = [
        pltpu.make_async_copy(source, target, in_sem.at[i])
        for i, (source, target) in enumerate(zip(sources, inputs))
    ]
    for i in FIRST + LATER:
        copies[i].start()
    run(wires, segments, chunk, copies, *inputs, *refs)


def run(
    wires,
    segments,
    chunk,
    copies,
    u_in, p_in, nodes_in, stiff_in, grad_in, mass_in, left_in, right_in, slots_in, live_in,
    u_out, p_out,
    u_ref, p_ref, mass_ref, rate_ref,
    c_hot, g_hot, c_back, g_back, x_back, e_back, cb_ref, gb_ref, xb_ref, count_ref, gram, nodes_ref, lists_ref, stiff_ref, scale_ref,
    part, field, pushed, c_send, c_recv, g_send, g_recv, x_send, x_recv,
    c_ssem, c_rsem, g_ssem, g_rsem, x_ssem, x_rsem,
):
    others = wires - 1
    direct = x_send.shape[0]
    blocks = e_back.shape[0]
    parts = u_in.shape[1]
    rows, wide = u_ref.shape
    pairs = slots_in.shape[3]
    ghosts = left_in.shape[2]
    elements, node_count = nodes_in.shape[2:]
    node_pad = gram.shape[0] // 2
    contact_row = elements
    ghost_row = contact_row + others * pairs // LANES
    me = lax.axis_index("wire")
    seg = lax.axis_index("len")
    has_prev = seg > 0
    has_next = seg < segments - 1
    half = ghosts // 2
    full, rest = divmod(half, wide)
    places = [(h * half + i * wide, wide, 2 * i + h, 0) for i in range(full) for h in range(2)]
    places += [(h * half + full * wide, rest, 2 * full, h * LANES) for h in range(2) if rest]
    groups = 2 * full + (rest > 0)
    mirrored = wires & (wires - 1) == 0

    def partner(d):
        if not mirrored:
            return lax.rem(me + (d + 1), wires)
        offset, other, bit = wires - 1 - d, me, 1
        while bit <= offset:
            if offset & bit:
                other = other + bit - 2 * bit * lax.rem(lax.div(me, bit), 2)
            bit *= 2
        return other

    def landing(d):
        return d if mirrored else others - 1 - d

    barrier = pltpu.get_barrier_semaphore()
    for d in range(others):
        pl.semaphore_signal(barrier, inc=1, device_id={"wire": partner(d)}, device_id_type=MESH)

    @pl.when(has_prev)
    def _():
        pl.semaphore_signal(barrier, inc=1, device_id={"len": seg - 1}, device_id_type=MESH)
        for d in range(direct):
            there = {"len": seg - 1, "wire": partner(d)}
            pl.semaphore_signal(barrier, inc=1, device_id=there, device_id_type=MESH)

    @pl.when(has_next)
    def _():
        pl.semaphore_signal(barrier, inc=1, device_id={"len": seg + 1}, device_id_type=MESH)
        for d in range(direct):
            there = {"len": seg + 1, "wire": partner(d)}
            pl.semaphore_signal(barrier, inc=1, device_id=there, device_id_type=MESH)

    def rows_of(width):
        return lax.broadcasted_iota(jnp.int32, (SUB, width), 0)

    def doubled(x):
        return x + pltpu.roll(x, 4, 0)

    def placed(values, base_ref, start, width, parts):
        high = values.astype(bf16).astype(f32)
        values = jnp.where(rows_of(width) < 4, high, values - high)
        which = base_ref[:, start : start + width]
        return jnp.concatenate([jnp.where(which == b, values, 0.0) for b in range(parts)], axis=0).astype(bf16)

    def put(values, back, base_ref, start, width, parts):
        return dot(placed(values, base_ref, start, width, parts), back[start : start + width, :])

    def match(slots):
        ids = lax.broadcasted_iota(jnp.int32, (wide, LANES), 0).astype(bf16)
        here = jnp.broadcast_to(slots.astype(f32), (2 * SUB, LANES)).astype(bf16)
        here = jnp.concatenate([here] * (wide // (2 * SUB)), axis=0)
        return jnp.where(ids == here, jnp.ones((), bf16), jnp.zeros((), bf16))

    def block_of(slots):
        return (slots * BLOCK_SCALE) >> BLOCK_SHIFT

    def spread_columns(columns, at):
        lanes = lax.broadcasted_iota(jnp.int32, (LANES, wide), 1).astype(bf16)
        here = jnp.broadcast_to(columns[:, at : at + 1], (LANES, wide))
        return jnp.where(lanes == here, jnp.ones((), bf16), jnp.zeros((), bf16))

    def fill(hot, base_ref, at, slots, live, row):
        count = slots.shape[1]
        which = block_of(slots)
        inside = slots - which * block_slots
        if live is not None:
            which = jnp.where(live > 0, which, -1)
        base_ref[:, at : at + count] = jnp.broadcast_to(which, (SUB, count))
        for start in range(0, count, LANES):
            here = inside[:, start : start + LANES]
            group, lane = divmod(at + start, hot.shape[2])
            hot[group, :, lane : lane + LANES] = match(here)
            at_row = row + (at + start) // LANES
            lists_ref[at_row : at_row + 1, :] = here.astype(f32)

    for i in FIRST:
        copies[i].wait()
    u_ref[...] = jnp.zeros_like(u_ref)
    p_ref[...] = jnp.zeros_like(p_ref)
    lists_ref[...] = jnp.zeros_like(lists_ref)
    for b in range(blocks):
        lanes = slice(b * block_slots, (b + 1) * block_slots)
        for c in range(parts):
            row = slice(b * SUB + c, b * SUB + c + 1)
            u_ref[row, :block_slots] = u_in[0, c, :, lanes]
    fill(g_hot, gb_ref, 0, left_in[0], None, ghost_row)
    fill(g_hot, gb_ref, ghosts, right_in[0], None, ghost_row)
    codes = []
    for side in range(2):
        for _, count, group, at in sorted(places):
            code = lax.broadcasted_iota(jnp.int32, (SUB, count), 1) + (wide * (side * groups + group + 1) + at)
            codes.append(code.astype(f32))
    codes = jnp.concatenate(codes, axis=1)
    last_row = (rows_of(wide) & 3) == 3
    codes = dot_nt(placed(codes, gb_ref, 0, 2 * ghosts, blocks), g_hot[0])
    for b in range(blocks):
        at = slice(b * SUB, (b + 1) * SUB)
        u_ref[at, :] = jnp.where(last_row, doubled(codes[at]), doubled(u_ref[at, :]))
    for d in range(others):
        fill(c_hot, cb_ref, d * pairs, slots_in[0, 0, pl.ds(partner(d), 1), :], live_in[0, 0, pl.ds(partner(d), 1), :], contact_row)

    @pl.when(jnp.logical_not(has_prev))
    def _():
        g_recv[:, 0] = jnp.zeros((ITERS,) + g_recv.shape[2:], f32)
        for d in range(direct):
            x_recv[:, d, 0] = jnp.zeros((ITERS,) + x_recv.shape[3:], f32)

    @pl.when(jnp.logical_not(has_next))
    def _():
        g_recv[:, 1] = jnp.zeros((ITERS,) + g_recv.shape[2:], f32)
        for d in range(direct):
            x_recv[:, d, 1] = jnp.zeros((ITERS,) + x_recv.shape[3:], f32)

    def prepare():
        for i in LATER:
            copies[i].wait()
        mass_ref[...] = jnp.zeros_like(mass_ref)
        for b in range(blocks):
            at = slice(b * SUB, (b + 1) * SUB)
            lanes = slice(b * block_slots, (b + 1) * block_slots)
            for c in range(parts):
                p_ref[b * SUB + c : b * SUB + c + 1, :block_slots] = p_in[0, c, :, lanes]
            p_ref[at, :] = jnp.where((rows_of(wide) & 3) < 3, doubled(p_ref[at, :]), u_ref[at, :])
            mass_ref[b * SUB + 3 : b * SUB + 4, :] = jnp.ones((1, wide), f32)
            mass_ref[b * SUB + 3 : b * SUB + 4, :block_slots] = mass_in[0, :, lanes]
            mass_ref[at, :] = doubled(mass_ref[at, :])
        op = grad_in[...]
        product = lax.dot_general(
            op, op, (((0,), (0,)), ((), ())), precision=lax.Precision.HIGHEST, preferred_element_type=f32
        )
        high = product.astype(bf16)
        low = (product - high.astype(f32)).astype(bf16)
        gram[...] = jnp.zeros_like(gram)
        for at in (0, node_pad):
            gram[at : at + node_count, :node_count] = high
            gram[at : at + node_count, node_pad : node_pad + node_count] = low
        nodes = jnp.concatenate([nodes_in[0, 0], jnp.full((elements, node_pad - node_count), -1, jnp.int32)], axis=1)
        lists_ref[:elements, :] = nodes.astype(f32)
        stiff_ref[...] = jnp.zeros_like(stiff_ref)
        stiff_ref[:, :elements] = jnp.broadcast_to(stiff_in[0], (stiff_ref.shape[0], elements))
        stiff_ref[...] = jnp.transpose(stiff_ref[...])
        first = rows_of(node_pad) < 4

        def both(source, one):
            here = jnp.broadcast_to(source[one : one + 1, :], (SUB, node_pad))
            return jnp.where(first, here, jnp.broadcast_to(source[one + 1 : one + 2, :], (SUB, node_pad)))

        for one in range(0, elements, 2):
            at = slice(one // 2 * SUB, (one // 2 + 1) * SUB)
            nodes_ref[at, :] = jnp.maximum(both(lists_ref, one), 0.0).astype(jnp.int32)
            scale_ref[at, :] = both(stiff_ref, one)
        columns = jnp.transpose(lists_ref[...]).astype(bf16)
        for one in range(elements):
            b, e = divmod(one, block_elements)
            e_back[b, e * node_pad : (e + 1) * node_pad, :] = spread_columns(columns, one)
        for i in range(others * pairs // LANES):
            c_back[i * LANES : (i + 1) * LANES, :] = spread_columns(columns, contact_row + i)

    def prepare_direct():
        for d in range(direct):
            live = live_in[0, 0, pl.ds(partner(d), 1), :]
            for k in range(pairs // LANES):
                h, at = divmod(k * LANES, pairs // 2)
                code = c_recv[0, d, 4 * h + 3 : 4 * h + 4, at : at + LANES]
                group = jnp.floor(code * (1.0 / wide))
                i = d * (pairs // LANES) + k
                lists_ref[i : i + 1, :] = code - wide * group
                alive = live[:, k * LANES : (k + 1) * LANES] > 0
                which = jnp.where(alive, group.astype(jnp.int32) - 1, -1)
                xb_ref[:, i * LANES : (i + 1) * LANES] = jnp.broadcast_to(which, (SUB, LANES))
        columns = jnp.transpose(lists_ref[...]).astype(bf16)
        for i in range(direct * pairs // LANES):
            x_back[i * LANES : (i + 1) * LANES, :] = spread_columns(columns, i)
        for i in range(2 * ghosts // LANES):
            g_back[i * LANES : (i + 1) * LANES, :] = spread_columns(columns, ghost_row + i)
        total = jnp.zeros((rows, wide), f32)
        width = c_hot.shape[2]
        for at in range(0, direct * pairs, width):
            total = total + put(jnp.ones((SUB, width), f32), c_back, cb_ref, at, width, blocks)
        for b in range(blocks):
            at = slice(b * SUB, (b + 1) * SUB)
            count_ref[at, :] = jnp.where((rows_of(wide) & 3) < 3, PENALTY * doubled(total[at]), 0.0)

    def entry():
        last = segments - 1
        pl.semaphore_wait(
            barrier, others + (direct + 1) * (lax.div(seg + last, segments) + lax.div(last - seg + last, segments))
        )

    row_all = lax.broadcasted_iota(jnp.int32, (rows, wide), 0) & (SUB - 1)
    low_all = row_all < 4

    def split(x):
        high = x.astype(bf16).astype(f32)
        return jnp.where(low_all, high, x - high).astype(bf16)

    def take(packed, hot, which):
        width = which.shape[1]
        picked = dot(packed, hot)
        total = jnp.zeros((SUB, width), f32)
        for b in range(blocks):
            total = jnp.where(which == b, picked[b * SUB : (b + 1) * SUB], total)
        return doubled(total)

    def take_list(packed, d, out_ref):
        width = c_hot.shape[2]
        for at in range(0, pairs // 2, width):
            both = []
            for start in (d * pairs + at, d * pairs + pairs // 2 + at):
                both.append(take(packed, c_hot[start // width], cb_ref[:, start : start + width]))
            out_ref[:, at : at + width] = jnp.where(rows_of(width) < 4, *both)

    def halves(here):
        turned = pltpu.roll(here, 4, 0)
        low = rows_of(here.shape[1]) < 4
        return jnp.where(low, here, turned), jnp.where(low, turned, here)

    def put_list(values, back, base_ref, d, parts, total):
        width = c_hot.shape[2]
        for at in range(0, pairs // 2, width):
            for h, here in enumerate(halves(values[:, at : at + width])):
                total = total + put(here, back, base_ref, d * pairs + h * (pairs // 2) + at, width, parts)
        return total

    def contact_copy(step, d):
        return pltpu.make_async_remote_copy(
            src_ref=c_send.at[d],
            dst_ref=c_recv.at[step, landing(d)],
            send_sem=c_ssem.at[d],
            recv_sem=c_rsem.at[step, landing(d)],
            device_id={"wire": partner(d)},
            device_id_type=MESH,
        )

    def contact_arrival(step, d):
        return pltpu.make_async_remote_copy(
            src_ref=c_send.at[d],
            dst_ref=c_recv.at[step, d],
            send_sem=c_ssem.at[d],
            recv_sem=c_rsem.at[step, d],
            device_id={"wire": partner(d)},
            device_id_type=MESH,
        )

    def ghost_copy(step, side):
        return pltpu.make_async_remote_copy(
            src_ref=g_send.at[side],
            dst_ref=g_recv.at[step, 1 - side],
            send_sem=g_ssem.at[side],
            recv_sem=g_rsem.at[step, 1 - side],
            device_id={"len": seg - 1 if side == 0 else seg + 1},
            device_id_type=MESH,
        )

    def ghost_arrival(step, side):
        return pltpu.make_async_remote_copy(
            src_ref=g_send.at[side],
            dst_ref=g_recv.at[step, side],
            send_sem=g_ssem.at[side],
            recv_sem=g_rsem.at[step, side],
            device_id={"len": seg - 1 if side == 0 else seg + 1},
            device_id_type=MESH,
        )

    def direct_copy(step, d, side):
        return pltpu.make_async_remote_copy(
            src_ref=x_send.at[d, side],
            dst_ref=x_recv.at[step, landing(d), 1 - side],
            send_sem=x_ssem.at[d, side],
            recv_sem=x_rsem.at[step, landing(d), 1 - side],
            device_id={"len": seg - 1 if side == 0 else seg + 1, "wire": partner(d)},
            device_id_type=MESH,
        )

    def direct_arrival(step, d, side):
        return pltpu.make_async_remote_copy(
            src_ref=x_send.at[d, side],
            dst_ref=x_recv.at[step, d, side],
            send_sem=x_ssem.at[d, side],
            recv_sem=x_rsem.at[step, d, side],
            device_id={"len": seg - 1 if side == 0 else seg + 1, "wire": partner(d)},
            device_id_type=MESH,
        )

    exists = (has_prev, has_next)
    far_first = sorted(range(others), key=lambda d: (1, 0).index(d) if d < 2 else d)

    def one_step(step, first):
        packed = split(u_ref[...])
        for d in range(others):
            take_list(packed, d, c_send.at[d])
        if first:
            entry()
            for d in far_first:
                contact_copy(step, d).start()
            prepare()
        else:
            for d in reversed(range(others)):
                contact_copy(step, d).start()
        for b in range(blocks):
            near, far = u_ref[b * SUB : (b + 1) * SUB, :LANES], u_ref[b * SUB : (b + 1) * SUB, LANES:]
            values = []
            for one in (2 * b, 2 * b + 1):
                slots = nodes_ref[one * SUB : (one + 1) * SUB, :]
                inside = slots & (LANES - 1)
                values.append(jnp.where(slots < LANES, lane_take(near, inside), lane_take(far, inside)))
            values = jnp.concatenate(values, axis=0)
            high = values.astype(bf16)
            at = slice(b * 2 * SUB, (b + 1) * 2 * SUB)
            field[at, :node_pad] = high
            field[at, node_pad:] = (values - high.astype(f32)).astype(bf16)
        reach = blocks * 2 * SUB // 4
        first16 = (lax.broadcasted_iota(jnp.int32, (2 * SUB, node_pad), 0) & (SUB - 1)) < 4
        for at in range(0, blocks * 2 * SUB, reach):
            out = dot(field[at : at + reach, :], gram[...])
            out = (out[:, :node_pad] + out[:, node_pad:]) * scale_ref[at : at + reach, :]
            for i in range(0, reach, 2 * SUB):
                b = (at + i) // (2 * SUB)
                pieces = []
                for j in range(2):
                    r = out[i + j * SUB : i + (j + 1) * SUB]
                    high = r.astype(bf16).astype(f32)
                    r = jnp.concatenate([high, r - high], axis=0)
                    pieces.append(jnp.where(first16, r, 0.0).astype(bf16))
                    pieces.append(jnp.where(first16, 0.0, r).astype(bf16))
                pushed[b * 2 * SUB : (b + 1) * 2 * SUB, :] = jnp.concatenate(pieces, axis=1)
        if not first:
            for d in range(direct):
                total = put_list(c_send[d], x_back, xb_ref, d, 2 * groups, jnp.zeros((2 * groups * SUB, wide), f32))
                total = [doubled(total[i * SUB : (i + 1) * SUB]) for i in range(2 * groups)]
                for side in range(2):
                    mine = total[side * groups : (side + 1) * groups]
                    for i in range(full):
                        x_send[d, side, :, i * wide : (i + 1) * wide] = jnp.where(rows_of(wide) < 4, mine[2 * i], mine[2 * i + 1])
                    if rest:
                        shared = jnp.where(rows_of(LANES) < 4, mine[2 * full][:, :LANES], mine[2 * full][:, LANES:])
                        x_send[d, side, :, full * wide :] = shared
            for side in range(2):

                @pl.when(exists[side])
                def _():
                    for d in range(direct):
                        direct_copy(step, d, side).start()

        for b in range(blocks):
            here = dot(pushed[b * 2 * SUB : (b + 1) * 2 * SUB, :], e_back[b])
            part[b * SUB : (b + 1) * SUB, :] = doubled(here[:SUB] + here[SUB:])

        spread = jnp.zeros((rows, wide), f32)
        for d in reversed(far_first if first else range(direct, others)):
            contact_arrival(step, d).wait_recv()
            spread = put_list(c_recv[step, d] - c_send[d], c_back, cb_ref, d, blocks, spread)
        inner = (rows_of(wide) & 3) < 3
        for b in range(blocks):
            at = slice(b * SUB, (b + 1) * SUB)
            if first:
                own = PENALTY * doubled(spread[at]) - part[at, :]
            else:
                own = -part[at, :] - count_ref[at, :] * u_ref[at, :]
            part[at, :] = jnp.where(inner, own, mass_ref[at, :])

        picked = take(split(part[...]), g_hot[0], gb_ref[...])
        for side in range(2):
            at = side * ghosts
            g_send[side] = jnp.where(rows_of(half) < 4, picked[:, at : at + half], picked[:, at + half : at + ghosts])
        for side in range(2):

            @pl.when(exists[side])
            def _():
                ghost_copy(step, side).start()

        if first:
            prepare_direct()
        else:
            spread = jnp.zeros((rows, wide), f32)
            for d in range(direct):
                contact_arrival(step, d).wait_recv()
                spread = put_list(c_recv[step, d], c_back, cb_ref, d, blocks, spread)
            for b in range(blocks):
                at = slice(b * SUB, (b + 1) * SUB)
                part[at, :] = part[at, :] + jnp.where(inner, PENALTY * doubled(spread[at]), 0.0)

        for side in range(2):

            @pl.when(exists[side])
            def _():
                ghost_arrival(step, side).wait_recv()
                for d in range(0 if first else direct):
                    direct_arrival(step, d, side).wait_recv()

        arrived = []
        for side in range(2):
            here = g_recv[step, side]
            if not first:
                crossed = sum(x_recv[step, d, side] for d in range(direct))
                here = here + jnp.where((rows_of(half) & 3) < 3, PENALTY * crossed, 0.0)
            arrived += halves(here)
        spread = put(jnp.concatenate(arrived, axis=1), g_back, gb_ref, 0, 2 * ghosts, blocks)
        for b in range(blocks):
            at = slice(b * SUB, (b + 1) * SUB)
            part[at, :] = part[at, :] + doubled(spread[at])

        if first:
            for b in range(blocks):
                mass = jnp.broadcast_to(part[b * SUB + 3 : b * SUB + 4, :], (SUB, wide))
                rate_ref[b * SUB : (b + 1) * SUB, :] = jnp.where(inner, TIME_SQUARE / mass, 0.0)

        now = u_ref[...]
        u_ref[...] = 2.0 * now - p_ref[...] + rate_ref[...] * part[...]
        p_ref[...] = now

        for d in range(others):
            contact_copy(step, d).wait_send()
        for side in range(2):

            @pl.when(exists[side])
            def _():
                ghost_copy(step, side).wait_send()
                for d in range(0 if first else direct):
                    direct_copy(step, d, side).wait_send()

    one_step(0, True)

    for step in range(1, ITERS):
        one_step(step, False)
    for b in range(blocks):
        lanes = slice(b * block_slots, (b + 1) * block_slots)
        for c in range(parts):
            row = slice(b * SUB + c, b * SUB + c + 1)
            u_out[0, c, :, lanes] = u_ref[row, :block_slots]
            p_out[0, c, :, lanes] = p_ref[row, :block_slots]


def hand_on(u_from, p_from, u_to, p_to):
    u_to[...] = u_from[...]
    p_to[...] = p_from[...]


def on_device(displacement, previous, element_nodes, *rest):
    left_ghost, contact_slots = rest[3], rest[5]
    node_count, elements = element_nodes.shape[2:]
    blocks = elements // block_elements
    wide = round_up(block_slots, 2 * LANES)
    node_pad = round_up(node_count, LANES)
    wires = lax.axis_size("wire")
    others = wires - 1
    rows = blocks * SUB
    pairs = contact_slots.shape[3]
    ghosts = left_ghost.shape[2]
    c_width = 512 if pairs % 1024 == 0 else pairs // 2
    direct = others
    groups = 2 * (ghosts // 2 // wide) + (ghosts // 2 % wide > 0)
    assert block_elements == 4 and node_pad == LANES and wide == 2 * LANES and blocks % 4 == 0
    assert elements + others * pairs // LANES + 2 * ghosts // LANES <= LANES
    assert direct > 0 and ghosts // 2 % wide in (0, LANES) and direct * pairs <= LANES * LANES
    assert wide * (2 * groups + 1) < 65536
    assert all((x * BLOCK_SCALE) >> BLOCK_SHIFT == x // block_slots for x in range(blocks * block_slots))

    vmem = pl.BlockSpec(memory_space=pltpu.VMEM)
    turned = jnp.swapaxes(displacement, 1, 2)
    args = (turned, jnp.swapaxes(previous, 1, 2), jnp.swapaxes(element_nodes, 2, 3), *rest)
    results = pl.pallas_call(
        functools.partial(step_kernel, wires, lax.axis_size("len"), 512),
        out_shape=[jax.ShapeDtypeStruct(turned.shape, f32)] * 2,
        in_specs=[pl.BlockSpec(memory_space=pl.ANY)] * len(args),
        out_specs=[vmem] * 2,
        scratch_shapes=[pltpu.VMEM(x.shape, x.dtype) for x in args]
        + [pltpu.SemaphoreType.DMA((len(args),))]
        + [
            pltpu.VMEM((rows, wide), f32),
            pltpu.VMEM((rows, wide), f32),
            pltpu.VMEM((rows, wide), f32),
            pltpu.VMEM((rows, wide), f32),
            pltpu.VMEM((others * pairs // c_width, wide, c_width), bf16),
            pltpu.VMEM((1, wide, 2 * ghosts), bf16),
            pltpu.VMEM((others * pairs, wide), bf16),
            pltpu.VMEM((2 * ghosts, wide), bf16),
            pltpu.VMEM((direct * pairs, wide), bf16),
            pltpu.VMEM((blocks, block_elements * node_pad, wide), bf16),
            pltpu.VMEM((SUB, others * pairs), jnp.int32),
            pltpu.VMEM((SUB, 2 * ghosts), jnp.int32),
            pltpu.VMEM((SUB, direct * pairs), jnp.int32),
            pltpu.VMEM((rows, wide), f32),
            pltpu.VMEM((2 * node_pad, 2 * node_pad), bf16),
            pltpu.VMEM((elements // 2 * SUB, node_pad), jnp.int32),
            pltpu.VMEM((LANES, LANES), f32),
            pltpu.VMEM((LANES, LANES), f32),
            pltpu.VMEM((elements // 2 * SUB, node_pad), f32),
            pltpu.VMEM((rows, wide), f32),
            pltpu.VMEM((elements // 2 * SUB, 2 * node_pad), bf16),
            pltpu.VMEM((blocks * 2 * SUB, block_elements * node_pad), bf16),
            pltpu.VMEM((others, SUB, pairs // 2), f32),
            pltpu.VMEM((ITERS, others, SUB, pairs // 2), f32),
            pltpu.VMEM((2, SUB, ghosts // 2), f32),
            pltpu.VMEM((ITERS, 2, SUB, ghosts // 2), f32),
            pltpu.VMEM((direct, 2, SUB, ghosts // 2), f32),
            pltpu.VMEM((ITERS, direct, 2, SUB, ghosts // 2), f32),
            pltpu.SemaphoreType.DMA((others,)),
            pltpu.SemaphoreType.DMA((ITERS, others)),
            pltpu.SemaphoreType.DMA((2,)),
            pltpu.SemaphoreType.DMA((ITERS, 2)),
            pltpu.SemaphoreType.DMA((direct, 2)),
            pltpu.SemaphoreType.DMA((ITERS, direct, 2)),
        ],
        compiler_params=pltpu.CompilerParams(
            collective_id=0, has_side_effects=True, vmem_limit_bytes=VMEM_BYTES
        ),
        name="steps",
    )(*args)
    results = pl.pallas_call(
        hand_on,
        out_shape=[jax.ShapeDtypeStruct(turned.shape, f32)] * 2,
        in_specs=[vmem] * 2,
        out_specs=[vmem] * 2,
        name="hand_on",
    )(*results)
    return tuple(jnp.swapaxes(x, 1, 2) for x in results)


def solution(mesh):
    four = P("len", "wire", None, None)
    three = P("len", "wire", None)
    return jax.shard_map(
        on_device,
        mesh=mesh,
        in_specs=(four, four, four, three, P(), three, three, three, four, four),
        out_specs=(four, four),
        check_vma=False,
    )
```

```python
import functools

import jax
import jax.numpy as jnp
from jax import lax
from jax.experimental import pallas as pl
from jax.experimental.pallas import tpu as pltpu
from jax.sharding import PartitionSpec as P

ITERS = 4
PENALTY = 4.0
TIME_SQUARE = 0.03
block_slots = 224
block_elements = 4
LANES = 128
ARGS = 10
VMEM_BYTES = 67_043_328
FIRST = (6, 7, 8, 9, 0)
LATER = (1, 2, 3, 4, 5)
BLOCK_SCALE, BLOCK_SHIFT = 4682, 20
SUB = 8
f32 = jnp.float32
bf16 = jnp.bfloat16
MESH = pl.DeviceIdType.MESH


def round_up(value, step):
    return -(-value // step) * step


def dot(a, b):
    return jnp.dot(a, b, preferred_element_type=f32)


def dot_nt(a, b):
    return lax.dot_general(a, b, (((1,), (1,)), ((), ())), preferred_element_type=f32)


def lane_take(values, lanes):
    return jnp.take_along_axis(values, lanes, axis=1, mode="promise_in_bounds")


def step_kernel(
    wires,
    segments,
    chunk,
    *refs,
):
    sources, refs = refs[:ARGS], refs[ARGS:]
    inputs, in_sem, refs = refs[2 : 2 + ARGS], refs[2 + ARGS], refs[:2] + refs[3 + ARGS :]
    copies = [
        pltpu.make_async_copy(source, target, in_sem.at[i])
        for i, (source, target) in enumerate(zip(sources, inputs))
    ]
    for i in FIRST + LATER:
        copies[i].start()
    run(wires, segments, chunk, copies, *inputs, *refs)


def run(
    wires,
    segments,
    chunk,
    copies,
    u_in, p_in, nodes_in, stiff_in, grad_in, mass_in, left_in, right_in, slots_in, live_in,
    u_out, p_out,
    u_ref, p_ref, mass_ref, rate_ref,
    c_hot, g_hot, c_back, g_back, x_back, e_back, cb_ref, gb_ref, xb_ref, count_ref, gram, nodes_ref, lists_ref, stiff_ref, scale_ref,
    part, field, pushed, c_send, c_recv, g_send, g_recv, x_send, x_recv,
    c_ssem, c_rsem, g_ssem, g_rsem, x_ssem, x_rsem,
):
    others = wires - 1
    direct = x_send.shape[0]
    blocks = e_back.shape[0]
    parts = u_in.shape[1]
    rows, wide = u_ref.shape
    pairs = slots_in.shape[3]
    ghosts = left_in.shape[2]
    elements, node_count = nodes_in.shape[2:]
    node_pad = gram.shape[0] // 2
    contact_row = elements
    ghost_row = contact_row + others * pairs // LANES
    me = lax.axis_index("wire")
    seg = lax.axis_index("len")
    has_prev = seg > 0
    has_next = seg < segments - 1
    half = ghosts // 2
    full, rest = divmod(half, wide)
    places = [(h * half + i * wide, wide, 2 * i + h, 0) for i in range(full) for h in range(2)]
    places += [(h * half + full * wide, rest, 2 * full, h * LANES) for h in range(2) if rest]
    groups = 2 * full + (rest > 0)
    mirrored = wires & (wires - 1) == 0

    def partner(d):
        if not mirrored:
            return lax.rem(me + (d + 1), wires)
        offset, other, bit = wires - 1 - d, me, 1
        while bit <= offset:
            if offset & bit:
                other = other + bit - 2 * bit * lax.rem(lax.div(me, bit), 2)
            bit *= 2
        return other

    def landing(d):
        return d if mirrored else others - 1 - d

    barrier = pltpu.get_barrier_semaphore()
    for d in range(others):
        pl.semaphore_signal(barrier, inc=1, device_id={"wire": partner(d)}, device_id_type=MESH)

    @pl.when(has_prev)
    def _():
        pl.semaphore_signal(barrier, inc=1, device_id={"len": seg - 1}, device_id_type=MESH)
        for d in range(direct):
            there = {"len": seg - 1, "wire": partner(d)}
            pl.semaphore_signal(barrier, inc=1, device_id=there, device_id_type=MESH)

    @pl.when(has_next)
    def _():
        pl.semaphore_signal(barrier, inc=1, device_id={"len": seg + 1}, device_id_type=MESH)
        for d in range(direct):
            there = {"len": seg + 1, "wire": partner(d)}
            pl.semaphore_signal(barrier, inc=1, device_id=there, device_id_type=MESH)

    def rows_of(width):
        return lax.broadcasted_iota(jnp.int32, (SUB, width), 0)

    def doubled(x):
        return x + pltpu.roll(x, 4, 0)

    def placed(values, base_ref, start, width, parts):
        high = values.astype(bf16).astype(f32)
        values = jnp.where(rows_of(width) < 4, high, values - high)
        which = base_ref[:, start : start + width]
        return jnp.concatenate([jnp.where(which == b, values, 0.0) for b in range(parts)], axis=0).astype(bf16)

    def put(values, back, base_ref, start, width, parts):
        return dot(placed(values, base_ref, start, width, parts), back[start : start + width, :])

    def match(slots):
        ids = lax.broadcasted_iota(jnp.int32, (wide, LANES), 0).astype(bf16)
        here = jnp.broadcast_to(slots.astype(f32), (2 * SUB, LANES)).astype(bf16)
        here = jnp.concatenate([here] * (wide // (2 * SUB)), axis=0)
        return jnp.where(ids == here, jnp.ones((), bf16), jnp.zeros((), bf16))

    def block_of(slots):
        return (slots * BLOCK_SCALE) >> BLOCK_SHIFT

    def spread_columns(columns, at):
        lanes = lax.broadcasted_iota(jnp.int32, (LANES, wide), 1).astype(bf16)
        here = jnp.broadcast_to(columns[:, at : at + 1], (LANES, wide))
        return jnp.where(lanes == here, jnp.ones((), bf16), jnp.zeros((), bf16))

    def fill(hot, base_ref, at, slots, live, row):
        count = slots.shape[1]
        which = block_of(slots)
        inside = slots - which * block_slots
        if live is not None:
            which = jnp.where(live > 0, which, -1)
        base_ref[:, at : at + count] = jnp.broadcast_to(which, (SUB, count))
        for start in range(0, count, LANES):
            here = inside[:, start : start + LANES]
            group, lane = divmod(at + start, hot.shape[2])
            hot[group, :, lane : lane + LANES] = match(here)
            at_row = row + (at + start) // LANES
            lists_ref[at_row : at_row + 1, :] = here.astype(f32)

    for i in FIRST:
        copies[i].wait()
    u_ref[...] = jnp.zeros_like(u_ref)
    p_ref[...] = jnp.zeros_like(p_ref)
    lists_ref[...] = jnp.zeros_like(lists_ref)
    for b in range(blocks):
        lanes = slice(b * block_slots, (b + 1) * block_slots)
        for c in range(parts):
            row = slice(b * SUB + c, b * SUB + c + 1)
            u_ref[row, :block_slots] = u_in[0, c, :, lanes]
    fill(g_hot, gb_ref, 0, left_in[0], None, ghost_row)
    fill(g_hot, gb_ref, ghosts, right_in[0], None, ghost_row)
    codes = []
    for side in range(2):
        for _, count, group, at in sorted(places):
            code = lax.broadcasted_iota(jnp.int32, (SUB, count), 1) + (wide * (side * groups + group + 1) + at)
            codes.append(code.astype(f32))
    codes = jnp.concatenate(codes, axis=1)
    last_row = (rows_of(wide) & 3) == 3
    codes = dot_nt(placed(codes, gb_ref, 0, 2 * ghosts, blocks), g_hot[0])
    for b in range(blocks):
        at = slice(b * SUB, (b + 1) * SUB)
        u_ref[at, :] = jnp.where(last_row, doubled(codes[at]), doubled(u_ref[at, :]))
    for d in range(others):
        fill(c_hot, cb_ref, d * pairs, slots_in[0, 0, pl.ds(partner(d), 1), :], live_in[0, 0, pl.ds(partner(d), 1), :], contact_row)

    @pl.when(jnp.logical_not(has_prev))
    def _():
        g_recv[:, 0] = jnp.zeros((ITERS,) + g_recv.shape[2:], f32)
        for d in range(direct):
            x_recv[:, d, 0] = jnp.zeros((ITERS,) + x_recv.shape[3:], f32)

    @pl.when(jnp.logical_not(has_next))
    def _():
        g_recv[:, 1] = jnp.zeros((ITERS,) + g_recv.shape[2:], f32)
        for d in range(direct):
            x_recv[:, d, 1] = jnp.zeros((ITERS,) + x_recv.shape[3:], f32)

    def prepare():
        for i in LATER:
            copies[i].wait()
        mass_ref[...] = jnp.zeros_like(mass_ref)
        for b in range(blocks):
            at = slice(b * SUB, (b + 1) * SUB)
            lanes = slice(b * block_slots, (b + 1) * block_slots)
            for c in range(parts):
                p_ref[b * SUB + c : b * SUB + c + 1, :block_slots] = p_in[0, c, :, lanes]
            p_ref[at, :] = jnp.where((rows_of(wide) & 3) < 3, doubled(p_ref[at, :]), u_ref[at, :])
            mass_ref[b * SUB + 3 : b * SUB + 4, :] = jnp.ones((1, wide), f32)
            mass_ref[b * SUB + 3 : b * SUB + 4, :block_slots] = mass_in[0, :, lanes]
            mass_ref[at, :] = doubled(mass_ref[at, :])
        op = grad_in[...]
        product = lax.dot_general(
            op, op, (((0,), (0,)), ((), ())), precision=lax.Precision.HIGHEST, preferred_element_type=f32
        )
        high = product.astype(bf16)
        low = (product - high.astype(f32)).astype(bf16)
        gram[...] = jnp.zeros_like(gram)
        for at in (0, node_pad):
            gram[at : at + node_count, :node_count] = high
            gram[at : at + node_count, node_pad : node_pad + node_count] = low
        nodes = jnp.concatenate([nodes_in[0, 0], jnp.full((elements, node_pad - node_count), -1, jnp.int32)], axis=1)
        lists_ref[:elements, :] = nodes.astype(f32)
        stiff_ref[...] = jnp.zeros_like(stiff_ref)
        stiff_ref[:, :elements] = jnp.broadcast_to(stiff_in[0], (stiff_ref.shape[0], elements))
        stiff_ref[...] = jnp.transpose(stiff_ref[...])
        first = rows_of(node_pad) < 4

        def both(source, one):
            here = jnp.broadcast_to(source[one : one + 1, :], (SUB, node_pad))
            return jnp.where(first, here, jnp.broadcast_to(source[one + 1 : one + 2, :], (SUB, node_pad)))

        for one in range(0, elements, 2):
            at = slice(one // 2 * SUB, (one // 2 + 1) * SUB)
            nodes_ref[at, :] = jnp.maximum(both(lists_ref, one), 0.0).astype(jnp.int32)
            scale_ref[at, :] = both(stiff_ref, one)
        columns = jnp.transpose(lists_ref[...]).astype(bf16)
        for one in range(elements):
            b, e = divmod(one, block_elements)
            e_back[b, e * node_pad : (e + 1) * node_pad, :] = spread_columns(columns, one)
        for i in range(others * pairs // LANES):
            c_back[i * LANES : (i + 1) * LANES, :] = spread_columns(columns, contact_row + i)

    def prepare_direct():
        for d in range(direct):
            live = live_in[0, 0, pl.ds(partner(d), 1), :]
            for k in range(pairs // LANES):
                h, at = divmod(k * LANES, pairs // 2)
                code = c_recv[0, d, 4 * h + 3 : 4 * h + 4, at : at + LANES]
                group = jnp.floor(code * (1.0 / wide))
                i = d * (pairs // LANES) + k
                lists_ref[i : i + 1, :] = code - wide * group
                alive = live[:, k * LANES : (k + 1) * LANES] > 0
                which = jnp.where(alive, group.astype(jnp.int32) - 1, -1)
                xb_ref[:, i * LANES : (i + 1) * LANES] = jnp.broadcast_to(which, (SUB, LANES))
        columns = jnp.transpose(lists_ref[...]).astype(bf16)
        for i in range(direct * pairs // LANES):
            x_back[i * LANES : (i + 1) * LANES, :] = spread_columns(columns, i)
        for i in range(2 * ghosts // LANES):
            g_back[i * LANES : (i + 1) * LANES, :] = spread_columns(columns, ghost_row + i)
        total = jnp.zeros((rows, wide), f32)
        width = c_hot.shape[2]
        for at in range(0, direct * pairs, width):
            total = total + put(jnp.ones((SUB, width), f32), c_back, cb_ref, at, width, blocks)
        for b in range(blocks):
            at = slice(b * SUB, (b + 1) * SUB)
            count_ref[at, :] = jnp.where((rows_of(wide) & 3) < 3, PENALTY * doubled(total[at]), 0.0)

    def entry():
        last = segments - 1
        pl.semaphore_wait(
            barrier, others + (direct + 1) * (lax.div(seg + last, segments) + lax.div(last - seg + last, segments))
        )

    row_all = lax.broadcasted_iota(jnp.int32, (rows, wide), 0) & (SUB - 1)
    low_all = row_all < 4

    def split(x):
        high = x.astype(bf16).astype(f32)
        return jnp.where(low_all, high, x - high).astype(bf16)

    def take(packed, hot, which):
        width = which.shape[1]
        picked = dot(packed, hot)
        total = jnp.zeros((SUB, width), f32)
        for b in range(blocks):
            total = jnp.where(which == b, picked[b * SUB : (b + 1) * SUB], total)
        return doubled(total)

    def take_list(packed, d, out_ref):
        width = c_hot.shape[2]
        for at in range(0, pairs // 2, width):
            both = []
            for start in (d * pairs + at, d * pairs + pairs // 2 + at):
                both.append(take(packed, c_hot[start // width], cb_ref[:, start : start + width]))
            out_ref[:, at : at + width] = jnp.where(rows_of(width) < 4, *both)

    def halves(here):
        turned = pltpu.roll(here, 4, 0)
        low = rows_of(here.shape[1]) < 4
        return jnp.where(low, here, turned), jnp.where(low, turned, here)

    def put_list(values, back, base_ref, d, parts, total):
        width = c_hot.shape[2]
        for at in range(0, pairs // 2, width):
            for h, here in enumerate(halves(values[:, at : at + width])):
                total = total + put(here, back, base_ref, d * pairs + h * (pairs // 2) + at, width, parts)
        return total

    def contact_copy(step, d):
        return pltpu.make_async_remote_copy(
            src_ref=c_send.at[d],
            dst_ref=c_recv.at[step, landing(d)],
            send_sem=c_ssem.at[d],
            recv_sem=c_rsem.at[step, landing(d)],
            device_id={"wire": partner(d)},
            device_id_type=MESH,
        )

    def contact_arrival(step, d):
        return pltpu.make_async_remote_copy(
            src_ref=c_send.at[d],
            dst_ref=c_recv.at[step, d],
            send_sem=c_ssem.at[d],
            recv_sem=c_rsem.at[step, d],
            device_id={"wire": partner(d)},
            device_id_type=MESH,
        )

    def ghost_copy(step, side):
        return pltpu.make_async_remote_copy(
            src_ref=g_send.at[side],
            dst_ref=g_recv.at[step, 1 - side],
            send_sem=g_ssem.at[side],
            recv_sem=g_rsem.at[step, 1 - side],
            device_id={"len": seg - 1 if side == 0 else seg + 1},
            device_id_type=MESH,
        )

    def ghost_arrival(step, side):
        return pltpu.make_async_remote_copy(
            src_ref=g_send.at[side],
            dst_ref=g_recv.at[step, side],
            send_sem=g_ssem.at[side],
            recv_sem=g_rsem.at[step, side],
            device_id={"len": seg - 1 if side == 0 else seg + 1},
            device_id_type=MESH,
        )

    def direct_copy(step, d, side):
        return pltpu.make_async_remote_copy(
            src_ref=x_send.at[d, side],
            dst_ref=x_recv.at[step, landing(d), 1 - side],
            send_sem=x_ssem.at[d, side],
            recv_sem=x_rsem.at[step, landing(d), 1 - side],
            device_id={"len": seg - 1 if side == 0 else seg + 1, "wire": partner(d)},
            device_id_type=MESH,
        )

    def direct_arrival(step, d, side):
        return pltpu.make_async_remote_copy(
            src_ref=x_send.at[d, side],
            dst_ref=x_recv.at[step, d, side],
            send_sem=x_ssem.at[d, side],
            recv_sem=x_rsem.at[step, d, side],
            device_id={"len": seg - 1 if side == 0 else seg + 1, "wire": partner(d)},
            device_id_type=MESH,
        )

    exists = (has_prev, has_next)
    far_first = sorted(range(others), key=lambda d: (1, 0).index(d) if d < 2 else d)

    def one_step(step, first):
        packed = split(u_ref[...])
        for d in range(others):
            take_list(packed, d, c_send.at[d])
        if first:
            entry()
            for d in far_first:
                contact_copy(step, d).start()
            prepare()
        else:
            for d in far_first:
                contact_copy(step, d).start()
        for b in range(blocks):
            near, far = u_ref[b * SUB : (b + 1) * SUB, :LANES], u_ref[b * SUB : (b + 1) * SUB, LANES:]
            values = []
            for one in (2 * b, 2 * b + 1):
                slots = nodes_ref[one * SUB : (one + 1) * SUB, :]
                inside = slots & (LANES - 1)
                values.append(jnp.where(slots < LANES, lane_take(near, inside), lane_take(far, inside)))
            values = jnp.concatenate(values, axis=0)
            high = values.astype(bf16)
            at = slice(b * 2 * SUB, (b + 1) * 2 * SUB)
            field[at, :node_pad] = high
            field[at, node_pad:] = (values - high.astype(f32)).astype(bf16)
        reach = blocks * 2 * SUB // 4
        first16 = (lax.broadcasted_iota(jnp.int32, (2 * SUB, node_pad), 0) & (SUB - 1)) < 4
        for at in range(0, blocks * 2 * SUB, reach):
            out = dot(field[at : at + reach, :], gram[...])
            out = (out[:, :node_pad] + out[:, node_pad:]) * scale_ref[at : at + reach, :]
            for i in range(0, reach, 2 * SUB):
                b = (at + i) // (2 * SUB)
                pieces = []
                for j in range(2):
                    r = out[i + j * SUB : i + (j + 1) * SUB]
                    high = r.astype(bf16).astype(f32)
                    r = jnp.concatenate([high, r - high], axis=0)
                    pieces.append(jnp.where(first16, r, 0.0).astype(bf16))
                    pieces.append(jnp.where(first16, 0.0, r).astype(bf16))
                pushed[b * 2 * SUB : (b + 1) * 2 * SUB, :] = jnp.concatenate(pieces, axis=1)
        if not first:
            for d in range(direct):
                total = put_list(c_send[d], x_back, xb_ref, d, 2 * groups, jnp.zeros((2 * groups * SUB, wide), f32))
                total = [doubled(total[i * SUB : (i + 1) * SUB]) for i in range(2 * groups)]
                for side in range(2):
                    mine = total[side * groups : (side + 1) * groups]
                    for i in range(full):
                        x_send[d, side, :, i * wide : (i + 1) * wide] = jnp.where(rows_of(wide) < 4, mine[2 * i], mine[2 * i + 1])
                    if rest:
                        shared = jnp.where(rows_of(LANES) < 4, mine[2 * full][:, :LANES], mine[2 * full][:, LANES:])
                        x_send[d, side, :, full * wide :] = shared
            for side in range(2):

                @pl.when(exists[side])
                def _():
                    for d in range(direct):
                        direct_copy(step, d, side).start()

        for b in range(blocks):
            here = dot(pushed[b * 2 * SUB : (b + 1) * 2 * SUB, :], e_back[b])
            part[b * SUB : (b + 1) * SUB, :] = doubled(here[:SUB] + here[SUB:])

        spread = jnp.zeros((rows, wide), f32)
        for d in reversed(far_first if first else range(direct, others)):
            contact_arrival(step, d).wait_recv()
            spread = put_list(c_recv[step, d] - c_send[d], c_back, cb_ref, d, blocks, spread)
        inner = (rows_of(wide) & 3) < 3
        for b in range(blocks):
            at = slice(b * SUB, (b + 1) * SUB)
            if first:
                own = PENALTY * doubled(spread[at]) - part[at, :]
            else:
                own = -part[at, :] - count_ref[at, :] * u_ref[at, :]
            part[at, :] = jnp.where(inner, own, mass_ref[at, :])

        picked = take(split(part[...]), g_hot[0], gb_ref[...])
        for side in range(2):
            at = side * ghosts
            g_send[side] = jnp.where(rows_of(half) < 4, picked[:, at : at + half], picked[:, at + half : at + ghosts])
        for side in range(2):

            @pl.when(exists[side])
            def _():
                ghost_copy(step, side).start()

        if first:
            prepare_direct()
        else:
            spread = jnp.zeros((rows, wide), f32)
            for d in range(direct):
                contact_arrival(step, d).wait_recv()
                spread = put_list(c_recv[step, d], c_back, cb_ref, d, blocks, spread)
            for b in range(blocks):
                at = slice(b * SUB, (b + 1) * SUB)
                part[at, :] = part[at, :] + jnp.where(inner, PENALTY * doubled(spread[at]), 0.0)

        for side in range(2):

            @pl.when(exists[side])
            def _():
                ghost_arrival(step, side).wait_recv()
                for d in range(0 if first else direct):
                    direct_arrival(step, d, side).wait_recv()

        arrived = []
        for side in range(2):
            here = g_recv[step, side]
            if not first:
                crossed = sum(x_recv[step, d, side] for d in range(direct))
                here = here + jnp.where((rows_of(half) & 3) < 3, PENALTY * crossed, 0.0)
            arrived += halves(here)
        spread = put(jnp.concatenate(arrived, axis=1), g_back, gb_ref, 0, 2 * ghosts, blocks)
        for b in range(blocks):
            at = slice(b * SUB, (b + 1) * SUB)
            part[at, :] = part[at, :] + doubled(spread[at])

        if first:
            for b in range(blocks):
                mass = jnp.broadcast_to(part[b * SUB + 3 : b * SUB + 4, :], (SUB, wide))
                rate_ref[b * SUB : (b + 1) * SUB, :] = jnp.where(inner, TIME_SQUARE / mass, 0.0)

        now = u_ref[...]
        u_ref[...] = 2.0 * now - p_ref[...] + rate_ref[...] * part[...]
        p_ref[...] = now

        for d in range(others):
            contact_copy(step, d).wait_send()
        for side in range(2):

            @pl.when(exists[side])
            def _():
                ghost_copy(step, side).wait_send()
                for d in range(0 if first else direct):
                    direct_copy(step, d, side).wait_send()

    one_step(0, True)

    for step in range(1, ITERS):
        one_step(step, False)
    for b in range(blocks):
        lanes = slice(b * block_slots, (b + 1) * block_slots)
        for c in range(parts):
            row = slice(b * SUB + c, b * SUB + c + 1)
            u_out[0, c, :, lanes] = u_ref[row, :block_slots]
            p_out[0, c, :, lanes] = p_ref[row, :block_slots]


def hand_on(u_from, p_from, u_to, p_to):
    u_to[...] = u_from[...]
    p_to[...] = p_from[...]


def on_device(displacement, previous, element_nodes, *rest):
    left_ghost, contact_slots = rest[3], rest[5]
    node_count, elements = element_nodes.shape[2:]
    blocks = elements // block_elements
    wide = round_up(block_slots, 2 * LANES)
    node_pad = round_up(node_count, LANES)
    wires = lax.axis_size("wire")
    others = wires - 1
    rows = blocks * SUB
    pairs = contact_slots.shape[3]
    ghosts = left_ghost.shape[2]
    c_width = 512 if pairs % 1024 == 0 else pairs // 2
    direct = others
    groups = 2 * (ghosts // 2 // wide) + (ghosts // 2 % wide > 0)
    assert block_elements == 4 and node_pad == LANES and wide == 2 * LANES and blocks % 4 == 0
    assert elements + others * pairs // LANES + 2 * ghosts // LANES <= LANES
    assert direct > 0 and ghosts // 2 % wide in (0, LANES) and direct * pairs <= LANES * LANES
    assert wide * (2 * groups + 1) < 65536
    assert all((x * BLOCK_SCALE) >> BLOCK_SHIFT == x // block_slots for x in range(blocks * block_slots))

    vmem = pl.BlockSpec(memory_space=pltpu.VMEM)
    turned = jnp.swapaxes(displacement, 1, 2)
    args = (turned, jnp.swapaxes(previous, 1, 2), jnp.swapaxes(element_nodes, 2, 3), *rest)
    results = pl.pallas_call(
        functools.partial(step_kernel, wires, lax.axis_size("len"), 512),
        out_shape=[jax.ShapeDtypeStruct(turned.shape, f32)] * 2,
        in_specs=[pl.BlockSpec(memory_space=pl.ANY)] * len(args),
        out_specs=[vmem] * 2,
        scratch_shapes=[pltpu.VMEM(x.shape, x.dtype) for x in args]
        + [pltpu.SemaphoreType.DMA((len(args),))]
        + [
            pltpu.VMEM((rows, wide), f32),
            pltpu.VMEM((rows, wide), f32),
            pltpu.VMEM((rows, wide), f32),
            pltpu.VMEM((rows, wide), f32),
            pltpu.VMEM((others * pairs // c_width, wide, c_width), bf16),
            pltpu.VMEM((1, wide, 2 * ghosts), bf16),
            pltpu.VMEM((others * pairs, wide), bf16),
            pltpu.VMEM((2 * ghosts, wide), bf16),
            pltpu.VMEM((direct * pairs, wide), bf16),
            pltpu.VMEM((blocks, block_elements * node_pad, wide), bf16),
            pltpu.VMEM((SUB, others * pairs), jnp.int32),
            pltpu.VMEM((SUB, 2 * ghosts), jnp.int32),
            pltpu.VMEM((SUB, direct * pairs), jnp.int32),
            pltpu.VMEM((rows, wide), f32),
            pltpu.VMEM((2 * node_pad, 2 * node_pad), bf16),
            pltpu.VMEM((elements // 2 * SUB, node_pad), jnp.int32),
            pltpu.VMEM((LANES, LANES), f32),
            pltpu.VMEM((LANES, LANES), f32),
            pltpu.VMEM((elements // 2 * SUB, node_pad), f32),
            pltpu.VMEM((rows, wide), f32),
            pltpu.VMEM((elements // 2 * SUB, 2 * node_pad), bf16),
            pltpu.VMEM((blocks * 2 * SUB, block_elements * node_pad), bf16),
            pltpu.VMEM((others, SUB, pairs // 2), f32),
            pltpu.VMEM((ITERS, others, SUB, pairs // 2), f32),
            pltpu.VMEM((2, SUB, ghosts // 2), f32),
            pltpu.VMEM((ITERS, 2, SUB, ghosts // 2), f32),
            pltpu.VMEM((direct, 2, SUB, ghosts // 2), f32),
            pltpu.VMEM((ITERS, direct, 2, SUB, ghosts // 2), f32),
            pltpu.SemaphoreType.DMA((others,)),
            pltpu.SemaphoreType.DMA((ITERS, others)),
            pltpu.SemaphoreType.DMA((2,)),
            pltpu.SemaphoreType.DMA((ITERS, 2)),
            pltpu.SemaphoreType.DMA((direct, 2)),
            pltpu.SemaphoreType.DMA((ITERS, direct, 2)),
        ],
        compiler_params=pltpu.CompilerParams(
            collective_id=0, has_side_effects=True, vmem_limit_bytes=VMEM_BYTES
        ),
        name="steps",
    )(*args)
    results = pl.pallas_call(
        hand_on,
        out_shape=[jax.ShapeDtypeStruct(turned.shape, f32)] * 2,
        in_specs=[vmem] * 2,
        out_specs=[vmem] * 2,
        name="hand_on",
    )(*results)
    return tuple(jnp.swapaxes(x, 1, 2) for x in results)


def solution(mesh):
    four = P("len", "wire", None, None)
    three = P("len", "wire", None)
    return jax.shard_map(
        on_device,
        mesh=mesh,
        in_specs=(four, four, four, three, P(), three, three, three, four, four),
        out_specs=(four, four),
        check_vma=False,
    )
```
